32 devices in a mesh: dp: 4 (over y, x), tm: 8 (over z, core).
Axes of the slice: x: 2, y: 2, z: 4, core: 2. Of those that a mesh axis runs over, the one named last changes fastest.
Arguments:
- frames: bfloat16 [16384, 1024], P(('dp', 'tm')), parts along dimension 0, may hold values from -6 to 6
- norm_gain1: float32 [1024], replicated, may hold values from 0.1 to 1.9
- w_qkv1: bfloat16 [1024, 1536], replicated, may hold values from -0.1875 to 0.1875
- log_decay: float32 [8, 16384], P(None, ('dp', 'tm')), parts along dimension 1, may hold values from -0.8 to 0, as said below
- head_gain: float32 [512], replicated, may hold values from 0.1 to 1.9
- w_out1: bfloat16 [512, 1024], replicated, may hold values from -0.25 to 0.25
- norm_gain2: float32 [1024], replicated, may hold values from 0.1 to 1.9
- w_qkv2: bfloat16 [1024, 1536], replicated, may hold values from -4 to 4
- window_ids: int32 [32, 2], P(('dp', 'tm')), parts along dimension 0, may hold values from -1 to 6, as said below
- w_out2: bfloat16 [512, 1024], replicated, may hold values from -0.25 to 0.25
Outputs:
- context: bfloat16 [16384, 1024], P(('dp', 'tm')), parts along dimension 0
The draws below stay inside these ranges and needn't reach their ends.
There are 4 independent parts, one for each index of `dp`. The reference program is written for one: setup_inputs(seed, part) draws one part's arguments, and reference() takes and returns one part's arrays. A program takes and returns all parts, laid end to end along the dimension named above; an argument that names none is the same for every part. Nothing has to cross between parts.
Inputs may be any that keep to these rules, and one draw needn't show every extreme that they name: `log_decay`: values are at most 0; in each head the decay varies over the frames. `window_ids`: row j holds distinct ids of blocks j - 3 to j - 1, or -1 for an empty slot; rows hold different numbers of ids, and some rows none. The last row lists 2 blocks, among them the blocks 1 and 3 before it.
All inputs are finite; a program needn't handle non-finite values.
Results may differ from the reference program's by a relative error of at most 0.0072.
Values may be sent and summed in bfloat16 or wider, within the bound.
A program may use at most 128 MiB of HBM per device.

```python
import math
import jax
import jax.numpy as jnp
from jax import lax

D = 1024
HALF_HEAD_COUNT = 8
HD = 64
BLK = 512
GROUP = 256
LIST = 2
REACH_BLOCKS = 3
UTTERANCE_FRAMES = 4096
NB = 8


def draw_log_decay(key, part):
    parallel_sequences = jax.random.split(key, 6)
    slow = jax.random.randint(parallel_sequences[0], (HALF_HEAD_COUNT, 1), 0, 10) < 5
    slow_rate = jax.random.uniform(parallel_sequences[1], (HALF_HEAD_COUNT, 1), jnp.float32, 0.2, 0.8) / UTTERANCE_FRAMES
    fast_rate = 1.0 / jax.random.uniform(parallel_sequences[2], (HALF_HEAD_COUNT, 1), jnp.float32, 30.0, 50.0)
    baseline_decay_rate = jnp.where(slow, slow_rate, fast_rate)
    coarse_estimate = jnp.exp(jax.random.uniform(parallel_sequences[3], (HALF_HEAD_COUNT, UTTERANCE_FRAMES), jnp.float32, math.log(0.5), math.log(2.0)))
    spike_position = jax.random.randint(parallel_sequences[4], (1, UTTERANCE_FRAMES), 0, UTTERANCE_FRAMES) < 3
    spike_magnitude = jnp.where(spike_position, jnp.log(jax.random.uniform(parallel_sequences[5], (HALF_HEAD_COUNT, UTTERANCE_FRAMES), jnp.float32, 0.5, 0.8)), 0.0)
    return (-baseline_decay_rate * coarse_estimate + spike_magnitude).astype(jnp.float32)


def draw_w_qkv2(key, part):
    parallel_sequences = jax.random.split(key, 1)
    width = HALF_HEAD_COUNT * HD
    weights = jnp.clip(jax.random.normal(parallel_sequences[0], (D, 3 * width), jnp.float32), -6.0, 6.0) * D ** (-0.5)
    return weights.astype(jnp.bfloat16)


def draw_window_ids(key, part):
    parallel_sequences = jax.random.split(key, 3)
    rows = jnp.arange(NB, dtype=jnp.int32)[:, None]
    offsets = jnp.arange(1, REACH_BLOCKS + 1, dtype=jnp.int32)[None, :]
    scores = jax.random.randint(parallel_sequences[0], (NB, REACH_BLOCKS), 0, 100000) * (2 * REACH_BLOCKS) + offsets
    last = rows == NB - 1
    far = (jax.random.randint(parallel_sequences[1], (NB, 1), 0, 2) == 1) | last
    scores = scores + jnp.where(far & (offsets == REACH_BLOCKS), 10000000, 0)
    scores = scores + jnp.where(last & (offsets == 1), 5000000, 0)
    order = jnp.argsort(-scores, axis=1, stable=True)[:, :LIST].astype(jnp.int32)
    chosen = order + 1
    counts = jax.random.randint(parallel_sequences[2], (NB, 1), 1, LIST + 1)
    counts = jnp.where(last, LIST, counts)
    slots = jnp.arange(LIST, dtype=jnp.int32)[None, :]
    ids = rows - chosen
    valid = (slots < counts) & (ids >= 0)
    return jnp.where(valid, ids, -1).astype(jnp.int32)


def level_of(stream_key, dims, cuts, smallest, top_value):
    level, own = 1.0, jax.random.fold_in(stream_key, 6)
    for axis_at, blocks in cuts:
        steps = jnp.exp(jax.random.uniform(jax.random.fold_in(own, axis_at), (blocks,), jnp.float32, smallest / len(cuts), top_value / len(cuts)))
        level = level * jnp.repeat(steps, dims[axis_at] // blocks).reshape([-1 if axis == axis_at else 1 for axis in range(len(dims))])
    return level


def centred(own_key, extent, scale, limit, cuts=(), kind=jnp.bfloat16):
    drawn = jax.random.normal(own_key, extent, jnp.float32) * scale
    if len(cuts) > 0:
        drawn = level_of(own_key, extent, cuts, -0.22, 0.18) * drawn
    return jnp.clip(drawn, min=-limit, max=limit).astype(kind)


def setup_inputs(seed: int = 0, part: int = 0) -> dict:
    key_list = jax.random.split(jax.random.key(seed), 11)
    part_splits = jax.random.split(jax.random.fold_in(key_list[10], part), 11)
    frames = centred(part_splits[0], (UTTERANCE_FRAMES, D), 1.0, 6.0, ((0, 8),))
    norm_gain1 = jnp.clip(1.0 + 0.18 * jax.random.normal(key_list[1], (D,), jnp.float32), 0.1, 1.9)
    w_qkv1 = centred(key_list[2], (D, 3 * HALF_HEAD_COUNT * HD), D ** -0.5, 0.1875)
    log_decay = draw_log_decay(jax.random.fold_in(jax.random.fold_in(key_list[10], part), 71), part)
    head_gain = jnp.clip(1.0 + 0.18 * jax.random.normal(key_list[4], (HALF_HEAD_COUNT * HD,), jnp.float32), 0.1, 1.9)
    w_out1 = centred(key_list[5], (HALF_HEAD_COUNT * HD, D), (HALF_HEAD_COUNT * HD) ** -0.5, 0.25)
    norm_gain2 = jnp.clip(1.0 + 0.18 * jax.random.normal(key_list[6], (D,), jnp.float32), 0.1, 1.9)
    w_qkv2 = draw_w_qkv2(jax.random.fold_in(key_list[10], 71), part)
    window_ids = draw_window_ids(jax.random.fold_in(jax.random.fold_in(key_list[10], part), 71), part)
    w_out2 = centred(key_list[9], (HALF_HEAD_COUNT * HD, D), (HALF_HEAD_COUNT * HD) ** -0.5, 0.25)
    return {"frames": frames, "norm_gain1": norm_gain1, "w_qkv1": w_qkv1, "log_decay": log_decay, "head_gain": head_gain, "w_out1": w_out1, "norm_gain2": norm_gain2, "w_qkv2": w_qkv2, "window_ids": window_ids, "w_out2": w_out2}


def rms_norm(values, gain):
    wide = values.astype(jnp.float32)
    scale = lax.rsqrt(lax.optimization_barrier(jnp.mean(wide * wide, axis=-1, keepdims=True)) + 1e-05)
    return (wide * scale * gain).astype(jnp.bfloat16)

def group_step(state, inputs):
    query, key_part, value, decay = inputs
    cumul = jnp.cumsum(decay, axis=0)
    scores = jnp.einsum('thd,shd->hts', query.astype(jnp.float32), key_part.astype(jnp.float32))
    trans = cumul.T
    diff = trans[:, :, None] - trans[:, None, :]
    length = decay.shape[0]
    causal = jnp.arange(length)[:, None] >= jnp.arange(length)[None, :]
    weight = jnp.where(causal[None], jnp.exp(jnp.minimum(diff, 0.0)), 0.0)
    mix = (scores * weight).astype(jnp.bfloat16)
    intra = jnp.einsum('hts,shd->thd', mix.astype(jnp.float32), value.astype(jnp.float32))
    scaled = query.astype(jnp.float32) * jnp.exp(cumul)[:, :, None]
    inter = jnp.einsum('thd,hde->the', scaled, state, precision=lax.Precision.HIGHEST)
    keyed = key_part.astype(jnp.float32) * jnp.exp(cumul[-1][None, :] - cumul)[:, :, None]
    update = jnp.einsum('shd,she->hde', keyed, value.astype(jnp.float32), precision=lax.Precision.HIGHEST)
    state = jnp.exp(cumul[-1])[:, None, None] * state + update
    return (state, intra + inter)

def reference(frames, norm_gain1, w_qkv1, log_decay, head_gain, w_out1, norm_gain2, w_qkv2, window_ids, w_out2):
    width = HALF_HEAD_COUNT * HD
    h_one = rms_norm(frames, norm_gain1)
    qkv = jnp.dot(h_one, w_qkv1, preferred_element_type=jnp.float32).astype(jnp.bfloat16)
    count = UTTERANCE_FRAMES // GROUP
    query = qkv[:, :width].reshape(count, GROUP, HALF_HEAD_COUNT, HD)
    key_part = qkv[:, width:2 * width].reshape(count, GROUP, HALF_HEAD_COUNT, HD)
    value = qkv[:, 2 * width:].reshape(count, GROUP, HALF_HEAD_COUNT, HD)
    decay = log_decay.T.reshape(count, GROUP, HALF_HEAD_COUNT)
    start = jnp.zeros((HALF_HEAD_COUNT, HD, HD), jnp.float32)
    final, lin = lax.scan(group_step, start, (query, key_part, value, decay))
    lin = lin.reshape(UTTERANCE_FRAMES, HALF_HEAD_COUNT, HD)
    normed = lin * lax.rsqrt(lax.optimization_barrier(jnp.mean(lin * lin, axis=-1, keepdims=True)) + 1e-06)
    y_one = (normed.reshape(UTTERANCE_FRAMES, width) * head_gain).astype(jnp.bfloat16)
    branch = jnp.dot(y_one, w_out1, preferred_element_type=jnp.float32)
    hidden1 = (frames.astype(jnp.float32) + branch).astype(jnp.bfloat16)
    h_two = rms_norm(hidden1, norm_gain2)
    qkv2 = jnp.dot(h_two, w_qkv2, preferred_element_type=jnp.float32).astype(jnp.bfloat16)
    q_blocks = qkv2[:, :width].reshape(NB, BLK, HALF_HEAD_COUNT, HD)
    k_blocks = qkv2[:, width:2 * width].reshape(NB, BLK, HALF_HEAD_COUNT, HD)
    v_blocks = qkv2[:, 2 * width:].reshape(NB, BLK, HALF_HEAD_COUNT, HD)
    causal = jnp.arange(BLK)[:, None] >= jnp.arange(BLK)[None, :]

    def one_block(index):
        ids = window_ids[index]
        valid = ids >= 0
        safe = jnp.clip(ids, 0, NB - 1).astype(jnp.int32)
        key_lines = jnp.concatenate([k_blocks[safe].reshape(LIST * BLK, HALF_HEAD_COUNT, HD), k_blocks[index]], axis=0)
        values = jnp.concatenate([v_blocks[safe].reshape(LIST * BLK, HALF_HEAD_COUNT, HD), v_blocks[index]], axis=0)
        listed = jnp.broadcast_to(jnp.repeat(valid, BLK)[None, :], (BLK, LIST * BLK))
        mask = jnp.concatenate([listed, causal], axis=1)
        scores = jnp.einsum('thd,shd->hts', q_blocks[index].astype(jnp.float32), key_lines.astype(jnp.float32)) * HD ** (-0.5)
        scores = jnp.where(mask[None], scores, -jnp.inf)
        top = lax.optimization_barrier(jnp.max(scores, axis=-1, keepdims=True))
        probs = jnp.exp(scores - top)
        total = lax.optimization_barrier(jnp.sum(probs, axis=-1))
        rounded = probs.astype(jnp.bfloat16)
        summed = jnp.einsum('hts,shd->thd', rounded.astype(jnp.float32), values.astype(jnp.float32))
        return (summed / total.T[:, :, None]).astype(jnp.bfloat16)
    attn = lax.map(one_block, jnp.arange(NB).astype(jnp.int32)).reshape(UTTERANCE_FRAMES, width)
    branch2 = jnp.dot(attn, w_out2, preferred_element_type=jnp.float32)
    return (hidden1.astype(jnp.float32) + branch2).astype(jnp.bfloat16)
```

```python
import functools

import jax
import jax.numpy as jnp
from jax import lax
from jax.experimental import pallas as pl
from jax.experimental.pallas import tpu as pltpu
from jax.sharding import PartitionSpec as P

MESH = pl.DeviceIdType.MESH
TILE = 256
LANES = 128
SCALE2 = 1.4426950408889634


def f32dot(a, b, dims=(((1,), (0,)), ((), ()))):
    return lax.dot_general(a, b, dims, preferred_element_type=jnp.float32)


def tile_at(index, size):
    return pl.ds(pl.multiple_of(index * size, size), size)


def norm_rows(src_ref, gain_ref, dst_ref):
    step = 128

    def body(i, carry):
        rows = tile_at(i, step)
        wide = src_ref[rows, :].astype(jnp.float32)
        scale = lax.rsqrt(jnp.mean(wide * wide, axis=-1, keepdims=True) + 1e-05)
        dst_ref[rows, :] = (wide * scale * gain_ref[...]).astype(jnp.bfloat16)
        return carry

    lax.fori_loop(0, src_ref.shape[0] // step, body, 0)


def layer_one(
    n,
    x_ref, g1_ref, w1_ref, ld_ref, hg_ref, wo_ref, g2_ref, w2_ref,
    hid_ref, qt_ref, kv_ref,
    h_s, qkv_s, y_s, run_s, runt_s, lin_s, x_s, ax_s, e_s, a_s, send_b, recv_b, send_sem, recv_sem,
):
    me = lax.axis_index("tm")
    rows = x_ref.shape[0]
    width = wo_ref.shape[0]
    heads = ld_ref.shape[0]
    pairs = width // LANES
    rounds = max(1, (n - 1).bit_length())
    dists = [1 << r for r in range(rounds)]

    barrier = pltpu.get_barrier_semaphore()
    for dist in dists:
        @pl.when(me + dist < n)
        def _():
            pl.semaphore_signal(barrier, inc=1, device_id={"tm": me + dist}, device_id_type=MESH)

        @pl.when(me >= dist)
        def _():
            pl.semaphore_signal(barrier, inc=1, device_id={"tm": me - dist}, device_id_type=MESH)

    norm_rows(x_ref, g1_ref, h_s)

    def project(j, carry):
        cols = tile_at(j, TILE)
        qkv_s[:, cols] = f32dot(h_s[...], w1_ref[:, cols]).astype(jnp.bfloat16)
        return carry

    lax.fori_loop(width // TILE, 3 * width // TILE, project, 0)

    upper = (
        lax.broadcasted_iota(jnp.int32, (rows, rows), 0)
        <= lax.broadcasted_iota(jnp.int32, (rows, rows), 1)
    ).astype(jnp.float32)
    run = lax.dot_general(
        ld_ref[...], upper, (((1,), (0,)), ((), ())),
        precision=lax.Precision.HIGHEST, preferred_element_type=jnp.float32,
    )
    run_s[...] = run
    runt_s[...] = run.T
    last = run[:, rows - 1 : rows]
    headsel = lax.broadcasted_iota(jnp.int32, (heads, width), 1) // (
        width // heads
    ) == lax.broadcasted_iota(jnp.int32, (heads, width), 0)
    a_row = jnp.sum(jnp.where(headsel, jnp.exp(last), 0.0), axis=0, keepdims=True)
    a_s[...] = a_row
    low = lax.broadcasted_iota(jnp.int32, (1, LANES), 1) < LANES // 2
    left_t = jnp.exp(last - run).T

    for p in range(pairs):
        cols = slice(p * LANES, (p + 1) * LANES)
        kcols = slice(width + p * LANES, width + (p + 1) * LANES)
        vcols = slice(2 * width + p * LANES, 2 * width + (p + 1) * LANES)
        decay = jnp.where(low, left_t[:, 2 * p : 2 * p + 1], left_t[:, 2 * p + 1 : 2 * p + 2])
        keyed = (qkv_s[:, kcols].astype(jnp.float32) * decay).T.astype(jnp.bfloat16)
        full = f32dot(keyed, qkv_s[:, vcols])
        e_s[:, cols] = jnp.where(low, full[: LANES // 2], full[LANES // 2 :])
    x_s[...] = jnp.zeros_like(x_s)
    ax_s[...] = jnp.ones_like(ax_s)

    def send(r, dist):
        w = e_s[...] + a_s[...] * x_s[...]
        aw = a_s[...] * ax_s[...]
        hi = aw.astype(jnp.bfloat16).astype(jnp.float32)
        lo = aw - hi
        row = lax.broadcasted_iota(jnp.int32, (16, width), 0)
        tail = jnp.where(row == 0, hi, jnp.where(row == 1, lo, 0.0))
        send_b[r, 0:64, :] = w.astype(jnp.bfloat16)
        send_b[r, 64:80, :] = tail.astype(jnp.bfloat16)

        @pl.when(me + dist < n)
        def _():
            copy_of(r, dist).start()

    def copy_of(r, dist):
        return pltpu.make_async_remote_copy(
            src_ref=send_b.at[r], dst_ref=recv_b.at[r],
            send_sem=send_sem.at[r], recv_sem=recv_sem.at[r],
            device_id={"tm": me + dist}, device_id_type=MESH,
        )

    def receive(r, dist):
        @pl.when(me >= dist)
        def _():
            copy_of(r, dist).wait_recv()
            got = recv_b[r].astype(jnp.float32)
            x_s[...] = x_s[...] + ax_s[...] * got[0:64]
            ax_s[...] = ax_s[...] * (got[64:65] + got[65:66])

    peers = [me + dist < n for dist in dists] + [me >= dist for dist in dists]
    pl.semaphore_wait(barrier, sum(peer.astype(jnp.int32) for peer in peers))

    def work_query():
        lax.fori_loop(0, width // TILE, project, 0)

    def work_pair(p):
        cols = slice(p * LANES, (p + 1) * LANES)
        kcols = slice(width + p * LANES, width + (p + 1) * LANES)
        vcols = slice(2 * width + p * LANES, 2 * width + (p + 1) * LANES)
        for first in range(0, rows, TILE):
            upto = first + TILE
            parts = []
            query = qkv_s[first:upto, cols]
            keys = qkv_s[0:upto, kcols]
            vals = qkv_s[0:upto, vcols]
            causal = lax.broadcasted_iota(jnp.int32, (TILE, upto), 0) + first >= (
                lax.broadcasted_iota(jnp.int32, (TILE, upto), 1)
            )
            for half in range(2):
                h = 2 * p + half
                keep = low if half == 0 else jnp.logical_not(low)
                mine = jnp.where(keep, query.astype(jnp.float32), 0.0).astype(jnp.bfloat16)
                scores = f32dot(mine, keys, (((1,), (1,)), ((), ())))
                diff = runt_s[first:upto, h : h + 1] - run_s[h : h + 1, 0:upto]
                weight = jnp.where(causal, jnp.exp(jnp.minimum(diff, 0.0)), 0.0)
                parts.append(f32dot((scores * weight).astype(jnp.bfloat16), vals))
            lin_s[first:upto, cols] = jnp.where(low, parts[0], parts[1])

    work = [work_query] + [functools.partial(work_pair, p) for p in range(pairs)]
    send(0, dists[0])
    for r, dist in enumerate(dists):
        take = 1 if r < rounds - 1 else len(work)
        if r == 1:
            take = 2
        for item in work[:take]:
            item()
        work = work[take:]
        receive(r, dist)
        if r + 1 < rounds:
            send(r + 1, dists[r + 1])
    for item in work:
        item()

    for p in range(pairs):
        cols = slice(p * LANES, (p + 1) * LANES)
        packed = x_s[:, cols]
        state = jnp.concatenate(
            [jnp.where(low, packed, 0.0), jnp.where(low, 0.0, packed)], axis=0
        ).astype(jnp.bfloat16)
        grow = jnp.exp(
            jnp.where(low, runt_s[:, 2 * p : 2 * p + 1], runt_s[:, 2 * p + 1 : 2 * p + 2])
        )
        scaled = (qkv_s[:, cols].astype(jnp.float32) * grow).astype(jnp.bfloat16)
        lin = lin_s[:, cols] + f32dot(scaled, state)
        square = lin * lin
        s0 = jnp.sum(jnp.where(low, square, 0.0), axis=-1, keepdims=True)
        s1 = jnp.sum(jnp.where(low, 0.0, square), axis=-1, keepdims=True)
        mean = jnp.where(low, s0, s1) * (1.0 / 64)
        y_s[:, cols] = (lin * lax.rsqrt(mean + 1e-06) * hg_ref[:, cols]).astype(jnp.bfloat16)

    def out_tile(j, carry):
        cols = tile_at(j, TILE)
        branch = f32dot(y_s[...], wo_ref[:, cols])
        hid_ref[:, cols] = (x_ref[:, cols].astype(jnp.float32) + branch).astype(jnp.bfloat16)
        return carry

    lax.fori_loop(0, x_ref.shape[1] // TILE, out_tile, 0)
    norm_rows(hid_ref, g2_ref, h_s)

    tiles = width // TILE

    def q_tile(j, carry):
        block = f32dot(h_s[...], w2_ref[:, tile_at(j, TILE)])
        qt_ref[tile_at(j, TILE), :] = block.T.astype(jnp.bfloat16)
        return carry

    def k_tile(j, carry):
        block = f32dot(h_s[...], w2_ref[:, tile_at(j + tiles, TILE)])
        kv_ref[0, :, tile_at(j, TILE)] = block.astype(jnp.bfloat16)
        return carry

    def v_tile(j, carry):
        block = f32dot(h_s[...], w2_ref[:, tile_at(j + 2 * tiles, TILE)])
        kv_ref[1, tile_at(j, TILE), :] = block.T.astype(jnp.bfloat16)
        return carry

    lax.fori_loop(0, tiles, k_tile, 0)
    lax.fori_loop(0, tiles, v_tile, 0)
    lax.fori_loop(0, tiles, q_tile, 0)
    for r, dist in enumerate(dists):
        @pl.when(me + dist < n)
        def _():
            copy_of(r, dist).wait_send()


def layer_two(
    n,
    qt_ref, kv_ref, hid_ref, bias_ref, wo_ref,
    out_ref,
    buf, m_s, l_s, acc_s, attn_s, own_send, relay_send, recv_sem,
):
    me = lax.axis_index("tm")
    width = wo_ref.shape[0]
    rows = hid_ref.shape[0]
    pairs = width // LANES
    even = lax.rem(me, 2) == 0
    odd = jnp.logical_not(even)

    barrier = pltpu.get_barrier_semaphore()
    links = [
        (jnp.logical_and(even, me >= 2), -2),
        (me >= 1, -1),
        (me + 1 < n, 1),
        (jnp.logical_and(even, me + 2 < n), 2),
    ]
    for cond, shift in links:
        @pl.when(cond)
        def _():
            pl.semaphore_signal(barrier, inc=1, device_id={"tm": me + shift}, device_id_type=MESH)
    pl.semaphore_wait(barrier, sum(cond.astype(jnp.int32) for cond, _ in links))

    def copy_of(src, slot, part, shift, sem):
        return pltpu.make_async_remote_copy(
            src_ref=src, dst_ref=buf.at[slot, part], send_sem=sem,
            recv_sem=recv_sem.at[slot, part],
            device_id={"tm": me + shift}, device_id_type=MESH,
        )

    to_next = me + 1 < n
    to_chip = jnp.logical_and(even, me + 2 < n)

    def own_next(part):
        return copy_of(kv_ref.at[part], 0, part, 1, own_send.at[0, part])

    def own_chip(part):
        return copy_of(kv_ref.at[part], 1, part, 2, own_send.at[1, part])

    relays = [
        (0, 1, 1, jnp.logical_and(even, jnp.logical_and(me >= 1, to_next))),
        (0, 2, 2, jnp.logical_and(to_chip, me >= 1)),
        (1, 2, 1, jnp.logical_and(even, jnp.logical_and(me >= 2, to_next))),
    ]

    def relay(index, part):
        source, slot, shift, _ = relays[index]
        return copy_of(buf.at[source, part], slot, part, shift, relay_send.at[index, part])

    for part in range(2):
        @pl.when(to_next)
        def _():
            own_next(part).start()

        @pl.when(to_chip)
        def _():
            own_chip(part).start()

    low = lax.broadcasted_iota(jnp.int32, (LANES, 1), 0) < LANES // 2
    scale = SCALE2 * 64 ** (-0.5)
    halves = rows // TILE

    def attend(k_ref, v_ref, first, bias):
        def body(i, carry):
            p = i // halves
            hq = lax.rem(i, halves)
            lanes = tile_at(hq, TILE)
            prow = tile_at(p, LANES)
            query = qt_ref[prow, lanes]
            keys = k_ref[:, prow]
            for half in range(2):
                keep = low if half == 0 else jnp.logical_not(low)
                mine = jnp.where(keep, query.astype(jnp.float32), 0.0).astype(jnp.bfloat16)
                s = f32dot(keys, mine) * scale
                if first:
                    seen = lax.broadcasted_iota(jnp.int32, s.shape, 0) <= (
                        lax.broadcasted_iota(jnp.int32, s.shape, 1) + hq * TILE
                    )
                    s = jnp.where(seen, s, -jnp.inf)
                top = jnp.max(s, axis=0, keepdims=True)
                h = 2 * p + half
                vrow = pl.ds(pl.multiple_of(h * 64, 64), 64)
                if first:
                    m_new = top
                    ref_top = top
                else:
                    m_old = m_s[h, :, lanes]
                    shift = bias[:, 0:TILE]
                    m_new = jnp.maximum(m_old, top + shift)
                    ref_top = m_new - shift
                    alpha = jnp.exp2(m_old - m_new)
                w = jnp.exp2(s - ref_top)
                total = jnp.sum(w, axis=0, keepdims=True)
                part = f32dot(v_ref[vrow, :], w.astype(jnp.bfloat16))
                if first:
                    l_s[h, :, lanes] = total
                    acc_s[vrow, lanes] = part
                else:
                    l_s[h, :, lanes] = l_s[h, :, lanes] * alpha + total
                    acc_s[vrow, lanes] = acc_s[vrow, lanes] * alpha + part
                m_s[h, :, lanes] = m_new
            return carry

        lax.fori_loop(0, pairs * halves, body, 0)

    attend(kv_ref.at[0], kv_ref.at[1], True, None)
    for slot in range(3):
        @pl.when(me >= slot + 1)
        def _():
            for part in range(2):
                copy_of(kv_ref.at[part], slot, part, 0, own_send.at[0, part]).wait_recv()
                for index in range(3):
                    if relays[index][0] == slot:
                        @pl.when(relays[index][3])
                        def _():
                            relay(index, part).start()
            attend(buf.at[slot, 0], buf.at[slot, 1], False, bias_ref[slot : slot + 1, :])

    for p in range(pairs):
        prow = slice(p * LANES, (p + 1) * LANES)
        inv = jnp.where(low, 1.0 / l_s[2 * p], 1.0 / l_s[2 * p + 1])
        attn_s[:, prow] = (acc_s[prow, :] * inv).T.astype(jnp.bfloat16)

    def out_tile(j, carry):
        cols = tile_at(j, TILE)
        branch = f32dot(attn_s[...], wo_ref[:, cols])
        out_ref[:, cols] = (hid_ref[:, cols].astype(jnp.float32) + branch).astype(jnp.bfloat16)
        return carry

    lax.fori_loop(0, hid_ref.shape[1] // TILE, out_tile, 0)
    for part in range(2):
        @pl.when(to_next)
        def _():
            own_next(part).wait_send()

        @pl.when(to_chip)
        def _():
            own_chip(part).wait_send()

        for index in range(3):
            @pl.when(relays[index][3])
            def _():
                relay(index, part).wait_send()


def local(
    frames, norm_gain1, w_qkv1, log_decay, head_gain, w_out1, norm_gain2, w_qkv2, window_ids, w_out2
):
    n = lax.axis_size("tm")
    rows, model = frames.shape
    width = w_out1.shape[0]
    heads = log_decay.shape[0]
    rounds = max(1, (n - 1).bit_length())
    vmem = pl.BlockSpec(memory_space=pltpu.VMEM)
    bf, f32 = jnp.bfloat16, jnp.float32
    hidden1, qt, kv = pl.pallas_call(
        functools.partial(layer_one, n),
        out_shape=(
            jax.ShapeDtypeStruct((rows, model), bf),
            jax.ShapeDtypeStruct((width, rows), bf),
            jax.ShapeDtypeStruct((2, width, rows), bf),
        ),
        in_specs=[vmem] * 8,
        out_specs=(vmem, vmem, vmem),
        scratch_shapes=[
            pltpu.VMEM((rows, model), bf),
            pltpu.VMEM((rows, 3 * width), bf),
            pltpu.VMEM((rows, width), bf),
            pltpu.VMEM((heads, rows), f32),
            pltpu.VMEM((rows, heads), f32),
            pltpu.VMEM((rows, width), f32),
            pltpu.VMEM((64, width), f32),
            pltpu.VMEM((1, width), f32),
            pltpu.VMEM((64, width), f32),
            pltpu.VMEM((1, width), f32),
            pltpu.VMEM((rounds, 80, width), bf),
            pltpu.VMEM((rounds, 80, width), bf),
            pltpu.SemaphoreType.DMA((rounds,)),
            pltpu.SemaphoreType.DMA((rounds,)),
        ],
        compiler_params=pltpu.CompilerParams(
            collective_id=0, has_side_effects=True, vmem_limit_bytes=48 * 2**20
        ),
    )(
        frames, norm_gain1.reshape(1, model), w_qkv1, log_decay, head_gain.reshape(1, width),
        w_out1, norm_gain2.reshape(1, model), w_qkv2,
    )
    wanted = lax.axis_index("tm") - jnp.arange(1, 9)
    listed = jnp.any((window_ids[0][None, :] == wanted[:, None]) & (wanted[:, None] >= 0), axis=1)
    bias = jnp.broadcast_to(jnp.where(listed, 0.0, -jnp.inf).astype(f32)[:, None], (8, rows))
    return pl.pallas_call(
        functools.partial(layer_two, n),
        out_shape=jax.ShapeDtypeStruct((rows, model), bf),
        in_specs=[vmem] * 5,
        out_specs=vmem,
        scratch_shapes=[
            pltpu.VMEM((3, 2, width, rows), bf),
            pltpu.VMEM((heads, 1, rows), f32),
            pltpu.VMEM((heads, 1, rows), f32),
            pltpu.VMEM((width, rows), f32),
            pltpu.VMEM((rows, width), bf),
            pltpu.SemaphoreType.DMA((2, 2)),
            pltpu.SemaphoreType.DMA((3, 2)),
            pltpu.SemaphoreType.DMA((3, 2)),
        ],
        compiler_params=pltpu.CompilerParams(
            collective_id=1, has_side_effects=True, vmem_limit_bytes=48 * 2**20
        ),
    )(qt, kv, hidden1, bias, w_out2)


def solution(mesh):
    placed = (
        P(("dp", "tm"), None),
        P(),
        P(),
        P(None, ("dp", "tm")),
        P(),
        P(),
        P(),
        P(),
        P(("dp", "tm"), None),
        P(),
    )
    return jax.shard_map(
        local, mesh=mesh, in_specs=placed, out_specs=P(("dp", "tm"), None), check_vma=False
    )
```

```python
import functools

import jax
import jax.numpy as jnp
from jax import lax
from jax.experimental import pallas as pl
from jax.experimental.pallas import tpu as pltpu
from jax.sharding import PartitionSpec as P

MESH = pl.DeviceIdType.MESH
TILE = 256
LANES = 128
SCALE2 = 1.4426950408889634


def f32dot(a, b, dims=(((1,), (0,)), ((), ()))):
    return lax.dot_general(a, b, dims, preferred_element_type=jnp.float32)


def tile_at(index, size):
    return pl.ds(pl.multiple_of(index * size, size), size)


def norm_rows(src_ref, gain_ref, dst_ref):
    step = 128

    def body(i, carry):
        rows = tile_at(i, step)
        wide = src_ref[rows, :].astype(jnp.float32)
        scale = lax.rsqrt(jnp.mean(wide * wide, axis=-1, keepdims=True) + 1e-05)
        dst_ref[rows, :] = (wide * scale * gain_ref[...]).astype(jnp.bfloat16)
        return carry

    lax.fori_loop(0, src_ref.shape[0] // step, body, 0)


def both_layers(
    n,
    x_hbm, g1_ref, w1_hbm, ld_ref, hg_ref, wo_hbm, g2_ref, w2_hbm, ids_ref, wp_hbm,
    out_ref,
    x_ref, w1_ref, wo_ref, w2_ref, wp_ref, hid_ref, qt_ref, k_own, v_own, k_buf, v_buf,
    m_s, l_s, acc_s, load_sem, own_send, relay_send, kv_recv,
    h_s, qkv_s, y_s, run_s, runt_s, lin_s, x_s, ax_s, e_s, a_s, send_b, recv_b, send_sem, recv_sem,
):
    me = lax.axis_index("tm")
    rows = x_ref.shape[0]
    width = wo_ref.shape[0]
    heads = ld_ref.shape[0]
    pairs = width // LANES
    rounds = max(2, (n - 1).bit_length())
    dists = [1 << r for r in range(rounds)]

    barrier = pltpu.get_barrier_semaphore()
    for dist in dists:
        @pl.when(me + dist < n)
        def _():
            pl.semaphore_signal(barrier, inc=1, device_id={"tm": me + dist}, device_id_type=MESH)

        @pl.when(me >= dist)
        def _():
            pl.semaphore_signal(barrier, inc=1, device_id={"tm": me - dist}, device_id_type=MESH)

    loads = [
        pltpu.make_async_copy(src, dst, load_sem.at[i])
        for i, (src, dst) in enumerate(
            [
                (x_hbm, x_ref),
                (w1_hbm.at[:, width:], w1_ref.at[:, width:]),
                (w1_hbm.at[:, :width], w1_ref.at[:, :width]),
                (wo_hbm, wo_ref),
                (w2_hbm, w2_ref),
                (wp_hbm, wp_ref),
            ]
        )
    ]
    for load in loads:
        load.start()
    loads[0].wait()
    norm_rows(x_ref, g1_ref, h_s)
    loads[1].wait()

    def project(j, carry):
        cols = tile_at(j, TILE)
        qkv_s[:, cols] = f32dot(h_s[...], w1_ref[:, cols]).astype(jnp.bfloat16)
        return carry

    lax.fori_loop(width // TILE, 3 * width // TILE, project, 0)

    upper = (
        lax.broadcasted_iota(jnp.int32, (rows, rows), 0)
        <= lax.broadcasted_iota(jnp.int32, (rows, rows), 1)
    ).astype(jnp.float32)
    run = lax.dot_general(
        ld_ref[...], upper, (((1,), (0,)), ((), ())),
        precision=lax.Precision.HIGHEST, preferred_element_type=jnp.float32,
    )
    run_s[...] = run
    runt_s[...] = run.T
    last = run[:, rows - 1 : rows]
    headsel = lax.broadcasted_iota(jnp.int32, (heads, width), 1) // (
        width // heads
    ) == lax.broadcasted_iota(jnp.int32, (heads, width), 0)
    a_row = jnp.sum(jnp.where(headsel, jnp.exp(last), 0.0), axis=0, keepdims=True)
    a_s[...] = a_row
    low = lax.broadcasted_iota(jnp.int32, (1, LANES), 1) < LANES // 2
    left_t = jnp.exp(last - run).T

    for p in range(pairs):
        cols = slice(p * LANES, (p + 1) * LANES)
        kcols = slice(width + p * LANES, width + (p + 1) * LANES)
        vcols = slice(2 * width + p * LANES, 2 * width + (p + 1) * LANES)
        decay = jnp.where(low, left_t[:, 2 * p : 2 * p + 1], left_t[:, 2 * p + 1 : 2 * p + 2])
        keyed = (qkv_s[:, kcols].astype(jnp.float32) * decay).T.astype(jnp.bfloat16)
        full = f32dot(keyed, qkv_s[:, vcols])
        e_s[:, cols] = jnp.where(low, full[: LANES // 2], full[LANES // 2 :])
    x_s[...] = jnp.zeros_like(x_s)
    ax_s[...] = jnp.ones_like(ax_s)

    def send(r, dist):
        w = e_s[...] + a_s[...] * x_s[...]
        aw = a_s[...] * ax_s[...]
        hi = aw.astype(jnp.bfloat16).astype(jnp.float32)
        lo = aw - hi
        row = lax.broadcasted_iota(jnp.int32, (16, width), 0)
        tail = jnp.where(row == 0, hi, jnp.where(row == 1, lo, 0.0))
        send_b[r, 0:64, :] = w.astype(jnp.bfloat16)
        send_b[r, 64:80, :] = tail.astype(jnp.bfloat16)

        @pl.when(me + dist < n)
        def _():
            copy_of(r, dist).start()

    def copy_of(r, dist):
        return pltpu.make_async_remote_copy(
            src_ref=send_b.at[r], dst_ref=recv_b.at[r],
            send_sem=send_sem.at[r], recv_sem=recv_sem.at[r],
            device_id={"tm": me + dist}, device_id_type=MESH,
        )

    def receive(r, dist):
        @pl.when(me >= dist)
        def _():
            copy_of(r, dist).wait_recv()
            got = recv_b[r].astype(jnp.float32)
            x_s[...] = x_s[...] + ax_s[...] * got[0:64]
            ax_s[...] = ax_s[...] * (got[64:65] + got[65:66])

    peers = [me + dist < n for dist in dists] + [me >= dist for dist in dists]
    pl.semaphore_wait(barrier, sum(peer.astype(jnp.int32) for peer in peers))

    def work_query():
        loads[2].wait()
        lax.fori_loop(0, width // TILE, project, 0)

    def work_pair(p):
        cols = slice(p * LANES, (p + 1) * LANES)
        kcols = slice(width + p * LANES, width + (p + 1) * LANES)
        vcols = slice(2 * width + p * LANES, 2 * width + (p + 1) * LANES)
        for first in range(0, rows, TILE):
            upto = first + TILE
            parts = []
            query = qkv_s[first:upto, cols]
            keys = qkv_s[0:upto, kcols]
            vals = qkv_s[0:upto, vcols]
            causal = lax.broadcasted_iota(jnp.int32, (TILE, upto), 0) + first >= (
                lax.broadcasted_iota(jnp.int32, (TILE, upto), 1)
            )
            for half in range(2):
                h = 2 * p + half
                keep = low if half == 0 else jnp.logical_not(low)
                mine = jnp.where(keep, query.astype(jnp.float32), 0.0).astype(jnp.bfloat16)
                scores = f32dot(mine, keys, (((1,), (1,)), ((), ())))
                diff = runt_s[first:upto, h : h + 1] - run_s[h : h + 1, 0:upto]
                weight = jnp.where(causal, jnp.exp(jnp.minimum(diff, 0.0)), 0.0)
                parts.append(f32dot((scores * weight).astype(jnp.bfloat16), vals))
            lin_s[first:upto, cols] = jnp.where(low, parts[0], parts[1])

    work = [work_query] + [functools.partial(work_pair, p) for p in range(pairs)]
    send(0, dists[0])
    for r, dist in enumerate(dists):
        take = 1 if r < rounds - 1 else len(work)
        if r == 1:
            take = 2
        for item in work[:take]:
            item()
        work = work[take:]
        receive(r, dist)
        if r + 1 < rounds:
            send(r + 1, dists[r + 1])
    for item in work:
        item()

    for p in range(pairs):
        cols = slice(p * LANES, (p + 1) * LANES)
        packed = x_s[:, cols]
        state = jnp.concatenate(
            [jnp.where(low, packed, 0.0), jnp.where(low, 0.0, packed)], axis=0
        ).astype(jnp.bfloat16)
        grow = jnp.exp(
            jnp.where(low, runt_s[:, 2 * p : 2 * p + 1], runt_s[:, 2 * p + 1 : 2 * p + 2])
        )
        scaled = (qkv_s[:, cols].astype(jnp.float32) * grow).astype(jnp.bfloat16)
        lin = lin_s[:, cols] + f32dot(scaled, state)
        square = lin * lin
        s0 = jnp.sum(jnp.where(low, square, 0.0), axis=-1, keepdims=True)
        s1 = jnp.sum(jnp.where(low, 0.0, square), axis=-1, keepdims=True)
        mean = jnp.where(low, s0, s1) * (1.0 / 64)
        y_s[:, cols] = (lin * lax.rsqrt(mean + 1e-06) * hg_ref[:, cols]).astype(jnp.bfloat16)

    def out_tile(j, carry):
        cols = tile_at(j, TILE)
        branch = f32dot(y_s[...], wo_ref[:, cols])
        hid_ref[:, cols] = (x_ref[:, cols].astype(jnp.float32) + branch).astype(jnp.bfloat16)
        return carry

    loads[3].wait()
    lax.fori_loop(0, x_ref.shape[1] // TILE, out_tile, 0)
    loads[4].wait()
    norm_rows(hid_ref, g2_ref, h_s)

    groups = width // TILE
    even = lax.rem(me, 2) == 0
    to_next = me + 1 < n
    to_chip = jnp.logical_and(even, me + 2 < n)
    relays = [
        (0, 1, 1, jnp.logical_and(even, jnp.logical_and(me >= 1, to_next))),
        (0, 2, 2, jnp.logical_and(to_chip, me >= 1)),
        (1, 2, 1, jnp.logical_and(even, jnp.logical_and(me >= 2, to_next))),
    ]

    def kv_copies(keys, vals, slot, g, shift, sems):
        return [
            pltpu.make_async_remote_copy(
                src_ref=src, dst_ref=dst.at[slot, g], send_sem=sems.at[i],
                recv_sem=kv_recv.at[slot, g, i],
                device_id={"tm": me + shift}, device_id_type=MESH,
            )
            for i, (src, dst) in enumerate([(keys, k_buf), (vals, v_buf)])
        ]

    def own_next(g):
        return kv_copies(k_own.at[g], v_own.at[g], 0, g, 1, own_send.at[0, g])

    def own_chip(g):
        return kv_copies(k_own.at[g], v_own.at[g], 1, g, 2, own_send.at[1, g])

    def relay(index, g):
        source, slot, shift, _ = relays[index]
        return kv_copies(
            k_buf.at[source, g], v_buf.at[source, g], slot, g, shift, relay_send.at[index, g]
        )

    for g in range(groups):
        lanes = slice(g * TILE, (g + 1) * TILE)
        kcols = slice(width + g * TILE, width + (g + 1) * TILE)
        vcols = slice(2 * width + g * TILE, 2 * width + (g + 1) * TILE)
        k_own[g] = f32dot(h_s[...], w2_ref[:, kcols]).astype(jnp.bfloat16)
        v_own[g] = f32dot(h_s[...], w2_ref[:, vcols]).T.astype(jnp.bfloat16)

        @pl.when(to_chip)
        def _():
            for copy in own_chip(g):
                copy.start()

        @pl.when(to_next)
        def _():
            for copy in own_next(g):
                copy.start()

    for g in range(groups):
        lanes = slice(g * TILE, (g + 1) * TILE)
        qt_ref[lanes, :] = f32dot(h_s[...], w2_ref[:, lanes]).T.astype(jnp.bfloat16)

    tall = lax.broadcasted_iota(jnp.int32, (LANES, 1), 0) < LANES // 2
    scale = SCALE2 * 64 ** (-0.5)
    halves = rows // TILE
    per_group = TILE // LANES

    def attend(k_ref, v_ref, g, first, bias):
        def body(i, carry):
            p = i // halves
            hq = lax.rem(i, halves)
            lanes = tile_at(hq, TILE)
            query = qt_ref[tile_at(p + g * per_group, LANES), lanes]
            keys = k_ref[:, tile_at(p, LANES)]
            for half in range(2):
                keep = tall if half == 0 else jnp.logical_not(tall)
                mine = jnp.where(keep, query.astype(jnp.float32), 0.0).astype(jnp.bfloat16)
                s = f32dot(keys, mine) * scale
                if first:
                    seen = lax.broadcasted_iota(jnp.int32, s.shape, 0) <= (
                        lax.broadcasted_iota(jnp.int32, s.shape, 1) + hq * TILE
                    )
                    s = jnp.where(seen, s, -jnp.inf)
                top = jnp.max(s, axis=0, keepdims=True)
                h = 2 * (p + g * per_group) + half
                vrow = pl.ds(pl.multiple_of((2 * p + half) * 64, 64), 64)
                arow = pl.ds(pl.multiple_of(h * 64, 64), 64)
                if first:
                    m_new = top
                    ref_top = top
                else:
                    m_old = m_s[h, :, lanes]
                    m_new = jnp.maximum(m_old, top + bias)
                    ref_top = m_new - bias
                    alpha = jnp.exp2(m_old - m_new)
                w = jnp.exp2(s - ref_top)
                total = jnp.sum(w, axis=0, keepdims=True)
                part = f32dot(v_ref[vrow, :], w.astype(jnp.bfloat16))
                if first:
                    l_s[h, :, lanes] = total
                    acc_s[arow, lanes] = part
                else:
                    l_s[h, :, lanes] = l_s[h, :, lanes] * alpha + total
                    acc_s[arow, lanes] = acc_s[arow, lanes] * alpha + part
                m_s[h, :, lanes] = m_new
            return carry

        lax.fori_loop(0, per_group * halves, body, 0)

    for g in range(groups):
        attend(k_own.at[g], v_own.at[g], g, True, None)

    order = [(slot, g) for g in range(groups) for slot in range(2)]
    order += [(2, g) for g in range(groups)]
    for slot, g in order:
        @pl.when(me >= slot + 1)
        def _():
            for copy in kv_copies(k_own.at[g], v_own.at[g], slot, g, 0, own_send.at[0, g]):
                copy.wait_recv()
            for index in (1, 0, 2):
                if relays[index][0] == slot:
                    @pl.when(relays[index][3])
                    def _():
                        for copy in relay(index, g):
                            copy.start()
            back = me - slot - 1
            listed = ids_ref[0, 0] == back
            for j in range(1, ids_ref.shape[1]):
                listed = jnp.logical_or(listed, ids_ref[0, j] == back)
            bias = jnp.where(listed, jnp.float32(0.0), jnp.float32(-jnp.inf))
            attend(k_buf.at[slot, g], v_buf.at[slot, g], g, False, bias)

    for p in range(pairs):
        prow = slice(p * LANES, (p + 1) * LANES)
        inv = jnp.where(tall, 1.0 / l_s[2 * p], 1.0 / l_s[2 * p + 1])
        y_s[:, prow] = (acc_s[prow, :] * inv).T.astype(jnp.bfloat16)

    def last_tile(j, carry):
        cols = tile_at(j, TILE)
        branch = f32dot(y_s[...], wp_ref[:, cols])
        out_ref[:, cols] = (hid_ref[:, cols].astype(jnp.float32) + branch).astype(jnp.bfloat16)
        return carry

    loads[5].wait()
    lax.fori_loop(0, hid_ref.shape[1] // TILE, last_tile, 0)

    def drain(copies):
        for copy in copies:
            copy.wait_send()

    for r, dist in enumerate(dists):
        @pl.when(me + dist < n)
        def _():
            copy_of(r, dist).wait_send()

    for g in range(groups):
        @pl.when(to_next)
        def _():
            drain(own_next(g))

        @pl.when(to_chip)
        def _():
            drain(own_chip(g))

        for index in range(3):
            @pl.when(relays[index][3])
            def _():
                drain(relay(index, g))


def local(
    frames, norm_gain1, w_qkv1, log_decay, head_gain, w_out1, norm_gain2, w_qkv2, window_ids, w_out2
):
    n = lax.axis_size("tm")
    rows, model = frames.shape
    width = w_out1.shape[0]
    heads = log_decay.shape[0]
    rounds = max(2, (n - 1).bit_length())
    groups = width // TILE
    vmem = pl.BlockSpec(memory_space=pltpu.VMEM)
    hbm = pl.BlockSpec(memory_space=pl.ANY)
    smem = pl.BlockSpec(memory_space=pltpu.SMEM)
    bf, f32 = jnp.bfloat16, jnp.float32
    return pl.pallas_call(
        functools.partial(both_layers, n),
        out_shape=jax.ShapeDtypeStruct((rows, model), bf),
        in_specs=[hbm, vmem, hbm, vmem, vmem, hbm, vmem, hbm, smem, hbm],
        out_specs=vmem,
        scratch_shapes=[
            pltpu.VMEM((rows, model), bf),
            pltpu.VMEM((model, 3 * width), bf),
            pltpu.VMEM((width, model), bf),
            pltpu.VMEM((model, 3 * width), bf),
            pltpu.VMEM((width, model), bf),
            pltpu.VMEM((rows, model), bf),
            pltpu.VMEM((width, rows), bf),
            pltpu.VMEM((groups, rows, TILE), bf),
            pltpu.VMEM((groups, TILE, rows), bf),
            pltpu.VMEM((3, groups, rows, TILE), bf),
            pltpu.VMEM((3, groups, TILE, rows), bf),
            pltpu.VMEM((heads, 1, rows), f32),
            pltpu.VMEM((heads, 1, rows), f32),
            pltpu.VMEM((width, rows), f32),
            pltpu.SemaphoreType.DMA((6,)),
            pltpu.SemaphoreType.DMA((2, groups, 2)),
            pltpu.SemaphoreType.DMA((3, groups, 2)),
            pltpu.SemaphoreType.DMA((3, groups, 2)),
            pltpu.VMEM((rows, model), bf),
            pltpu.VMEM((rows, 3 * width), bf),
            pltpu.VMEM((rows, width), bf),
            pltpu.VMEM((heads, rows), f32),
            pltpu.VMEM((rows, heads), f32),
            pltpu.VMEM((rows, width), f32),
            pltpu.VMEM((64, width), f32),
            pltpu.VMEM((1, width), f32),
            pltpu.VMEM((64, width), f32),
            pltpu.VMEM((1, width), f32),
            pltpu.VMEM((rounds, 80, width), bf),
            pltpu.VMEM((rounds, 80, width), bf),
            pltpu.SemaphoreType.DMA((rounds,)),
            pltpu.SemaphoreType.DMA((rounds,)),
        ],
        compiler_params=pltpu.CompilerParams(
            collective_id=0, has_side_effects=True, vmem_limit_bytes=60 * 2**20
        ),
    )(
        frames, norm_gain1.reshape(1, model), w_qkv1, log_decay, head_gain.reshape(1, width),
        w_out1, norm_gain2.reshape(1, model), w_qkv2, window_ids, w_out2,
    )


def solution(mesh):
    placed = (
        P(("dp", "tm"), None),
        P(),
        P(),
        P(None, ("dp", "tm")),
        P(),
        P(),
        P(),
        P(),
        P(("dp", "tm"), None),
        P(),
    )
    return jax.shard_map(
        local, mesh=mesh, in_specs=placed, out_specs=P(("dp", "tm"), None), check_vma=False
    )
```

```python
import functools

import jax
import jax.numpy as jnp
from jax import lax
from jax.experimental import pallas as pl
from jax.experimental.pallas import tpu as pltpu
from jax.sharding import PartitionSpec as P

MESH = pl.DeviceIdType.MESH
TILE = 256
LANES = 128
SCALE2 = 1.4426950408889634


def f32dot(a, b, dims=(((1,), (0,)), ((), ()))):
    return lax.dot_general(a, b, dims, preferred_element_type=jnp.float32)


def tile_at(index, size):
    return pl.ds(pl.multiple_of(index * size, size), size)


def norm_rows(src_ref, gain_ref, dst_ref):
    step = 128

    def body(i, carry):
        rows = tile_at(i, step)
        wide = src_ref[rows, :].astype(jnp.float32)
        scale = lax.rsqrt(jnp.mean(wide * wide, axis=-1, keepdims=True) + 1e-05)
        dst_ref[rows, :] = (wide * scale * gain_ref[...]).astype(jnp.bfloat16)
        return carry

    lax.fori_loop(0, src_ref.shape[0] // step, body, 0)


def both_layers(
    n,
    x_hbm, g1_ref, w1_hbm, ld_ref, hg_ref, wo_hbm, g2_ref, w2_hbm, ids_ref, wp_hbm,
    out_ref,
    x_ref, w1_ref, wo_ref, w2_ref, wp_ref, hid_ref, qt_ref, k_own, v_own, k_buf, v_buf,
    m_s, l_s, acc_s, load_sem, own_send, relay_send, kv_recv,
    q_far, o_send, o_recv, st_send, st_recv, far_send, far_recv,
    h_s, qkv_s, y_s, run_s, runt_s, lin_s, x_s, ax_s, e_s, a_s, send_b, recv_b, send_sem, recv_sem,
):
    me = lax.axis_index("tm")
    rows = x_ref.shape[0]
    width = wo_ref.shape[0]
    heads = ld_ref.shape[0]
    pairs = width // LANES
    rounds = max(2, (n - 1).bit_length())
    dists = [1 << r for r in range(rounds)]

    barrier = pltpu.get_barrier_semaphore()
    for dist in dists:
        @pl.when(me + dist < n)
        def _():
            pl.semaphore_signal(barrier, inc=1, device_id={"tm": me + dist}, device_id_type=MESH)

        @pl.when(me >= dist)
        def _():
            pl.semaphore_signal(barrier, inc=1, device_id={"tm": me - dist}, device_id_type=MESH)

    loads = [
        pltpu.make_async_copy(src, dst, load_sem.at[i])
        for i, (src, dst) in enumerate(
            [
                (x_hbm, x_ref),
                (w1_hbm.at[:, width:], w1_ref.at[:, width:]),
                (w1_hbm.at[:, :width], w1_ref.at[:, :width]),
                (wo_hbm, wo_ref),
                (w2_hbm, w2_ref),
                (wp_hbm, wp_ref),
            ]
        )
    ]
    for load in loads:
        load.start()
    loads[0].wait()
    norm_rows(x_ref, g1_ref, h_s)
    loads[1].wait()

    def project(j, carry):
        cols = tile_at(j, TILE)
        qkv_s[:, cols] = f32dot(h_s[...], w1_ref[:, cols]).astype(jnp.bfloat16)
        return carry

    lax.fori_loop(width // TILE, 3 * width // TILE, project, 0)

    upper = (
        lax.broadcasted_iota(jnp.int32, (rows, rows), 0)
        <= lax.broadcasted_iota(jnp.int32, (rows, rows), 1)
    ).astype(jnp.float32)
    run = lax.dot_general(
        ld_ref[...], upper, (((1,), (0,)), ((), ())),
        precision=lax.Precision.HIGHEST, preferred_element_type=jnp.float32,
    )
    run_s[...] = run
    runt_s[...] = run.T
    last = run[:, rows - 1 : rows]
    headsel = lax.broadcasted_iota(jnp.int32, (heads, width), 1) // (
        width // heads
    ) == lax.broadcasted_iota(jnp.int32, (heads, width), 0)
    a_row = jnp.sum(jnp.where(headsel, jnp.exp(last), 0.0), axis=0, keepdims=True)
    a_s[...] = a_row
    low = lax.broadcasted_iota(jnp.int32, (1, LANES), 1) < LANES // 2
    left_t = jnp.exp(last - run).T

    for p in range(pairs):
        cols = slice(p * LANES, (p + 1) * LANES)
        kcols = slice(width + p * LANES, width + (p + 1) * LANES)
        vcols = slice(2 * width + p * LANES, 2 * width + (p + 1) * LANES)
        decay = jnp.where(low, left_t[:, 2 * p : 2 * p + 1], left_t[:, 2 * p + 1 : 2 * p + 2])
        keyed = (qkv_s[:, kcols].astype(jnp.float32) * decay).T.astype(jnp.bfloat16)
        full = f32dot(keyed, qkv_s[:, vcols])
        e_s[:, cols] = jnp.where(low, full[: LANES // 2], full[LANES // 2 :])
    x_s[...] = jnp.zeros_like(x_s)
    ax_s[...] = jnp.ones_like(ax_s)

    def send(r, dist):
        w = e_s[...] + a_s[...] * x_s[...]
        aw = a_s[...] * ax_s[...]
        hi = aw.astype(jnp.bfloat16).astype(jnp.float32)
        lo = aw - hi
        row = lax.broadcasted_iota(jnp.int32, (16, width), 0)
        tail = jnp.where(row == 0, hi, jnp.where(row == 1, lo, 0.0))
        send_b[r, 0:64, :] = w.astype(jnp.bfloat16)
        send_b[r, 64:80, :] = tail.astype(jnp.bfloat16)

        @pl.when(me + dist < n)
        def _():
            copy_of(r, dist).start()

    def copy_of(r, dist):
        return pltpu.make_async_remote_copy(
            src_ref=send_b.at[r], dst_ref=recv_b.at[r],
            send_sem=send_sem.at[r], recv_sem=recv_sem.at[r],
            device_id={"tm": me + dist}, device_id_type=MESH,
        )

    def receive(r, dist):
        @pl.when(me >= dist)
        def _():
            copy_of(r, dist).wait_recv()
            got = recv_b[r].astype(jnp.float32)
            x_s[...] = x_s[...] + ax_s[...] * got[0:64]
            ax_s[...] = ax_s[...] * (got[64:65] + got[65:66])

    peers = [me + dist < n for dist in dists] + [me >= dist for dist in dists]
    pl.semaphore_wait(barrier, sum(peer.astype(jnp.int32) for peer in peers))

    def work_query():
        loads[2].wait()
        lax.fori_loop(0, width // TILE, project, 0)

    def work_pair(p):
        cols = slice(p * LANES, (p + 1) * LANES)
        kcols = slice(width + p * LANES, width + (p + 1) * LANES)
        vcols = slice(2 * width + p * LANES, 2 * width + (p + 1) * LANES)
        for first in range(0, rows, TILE):
            upto = first + TILE
            parts = []
            query = qkv_s[first:upto, cols]
            keys = qkv_s[0:upto, kcols]
            vals = qkv_s[0:upto, vcols]
            causal = lax.broadcasted_iota(jnp.int32, (TILE, upto), 0) + first >= (
                lax.broadcasted_iota(jnp.int32, (TILE, upto), 1)
            )
            for half in range(2):
                h = 2 * p + half
                keep = low if half == 0 else jnp.logical_not(low)
                mine = jnp.where(keep, query.astype(jnp.float32), 0.0).astype(jnp.bfloat16)
                scores = f32dot(mine, keys, (((1,), (1,)), ((), ())))
                diff = runt_s[first:upto, h : h + 1] - run_s[h : h + 1, 0:upto]
                weight = jnp.where(causal, jnp.exp(jnp.minimum(diff, 0.0)), 0.0)
                parts.append(f32dot((scores * weight).astype(jnp.bfloat16), vals))
            lin_s[first:upto, cols] = jnp.where(low, parts[0], parts[1])

    work = [work_query] + [functools.partial(work_pair, p) for p in range(pairs)]
    send(0, dists[0])
    for r, dist in enumerate(dists):
        take = 1 if r < rounds - 1 else len(work)
        if r == 1:
            take = 2
        for item in work[:take]:
            item()
        work = work[take:]
        receive(r, dist)
        if r + 1 < rounds:
            send(r + 1, dists[r + 1])
    for item in work:
        item()

    for p in range(pairs):
        cols = slice(p * LANES, (p + 1) * LANES)
        packed = x_s[:, cols]
        state = jnp.concatenate(
            [jnp.where(low, packed, 0.0), jnp.where(low, 0.0, packed)], axis=0
        ).astype(jnp.bfloat16)
        grow = jnp.exp(
            jnp.where(low, runt_s[:, 2 * p : 2 * p + 1], runt_s[:, 2 * p + 1 : 2 * p + 2])
        )
        scaled = (qkv_s[:, cols].astype(jnp.float32) * grow).astype(jnp.bfloat16)
        lin = lin_s[:, cols] + f32dot(scaled, state)
        square = lin * lin
        s0 = jnp.sum(jnp.where(low, square, 0.0), axis=-1, keepdims=True)
        s1 = jnp.sum(jnp.where(low, 0.0, square), axis=-1, keepdims=True)
        mean = jnp.where(low, s0, s1) * (1.0 / 64)
        y_s[:, cols] = (lin * lax.rsqrt(mean + 1e-06) * hg_ref[:, cols]).astype(jnp.bfloat16)

    def out_tile(j, carry):
        cols = tile_at(j, TILE)
        branch = f32dot(y_s[...], wo_ref[:, cols])
        hid_ref[:, cols] = (x_ref[:, cols].astype(jnp.float32) + branch).astype(jnp.bfloat16)
        return carry

    loads[3].wait()
    lax.fori_loop(0, x_ref.shape[1] // TILE, out_tile, 0)
    loads[4].wait()
    norm_rows(hid_ref, g2_ref, h_s)

    groups = width // TILE
    even = lax.rem(me, 2) == 0
    to_next = me + 1 < n
    to_chip = jnp.logical_and(even, me + 2 < n)
    relays = [
        (0, 1, 1, jnp.logical_and(even, jnp.logical_and(me >= 1, to_next))),
        (1, 2, 1, jnp.logical_and(even, jnp.logical_and(me >= 2, to_next))),
    ]
    helps = jnp.logical_and(to_chip, me >= 1)
    helped = jnp.logical_and(even, me >= 3)

    def query_back(g):
        return pltpu.make_async_remote_copy(
            src_ref=qt_ref.at[tile_at(g, TILE)], dst_ref=q_far.at[tile_at(g, TILE)],
            send_sem=far_send.at[g, 0], recv_sem=far_recv.at[g, 0],
            device_id={"tm": me - 2}, device_id_type=MESH,
        )

    def partial_on(g):
        return [
            pltpu.make_async_remote_copy(
                src_ref=src.at[g], dst_ref=dst.at[g],
                send_sem=far_send.at[g, i], recv_sem=far_recv.at[g, i],
                device_id={"tm": me + 2}, device_id_type=MESH,
            )
            for i, (src, dst) in [(1, (o_send, o_recv)), (2, (st_send, st_recv))]
        ]

    def kv_copies(keys, vals, slot, g, shift, sems):
        return [
            pltpu.make_async_remote_copy(
                src_ref=src, dst_ref=dst.at[slot, g], send_sem=sems.at[i],
                recv_sem=kv_recv.at[slot, g, i],
                device_id={"tm": me + shift}, device_id_type=MESH,
            )
            for i, (src, dst) in enumerate([(keys, k_buf), (vals, v_buf)])
        ]

    def own_next(g):
        return kv_copies(k_own.at[g], v_own.at[g], 0, g, 1, own_send.at[0, g])

    def own_chip(g):
        return kv_copies(k_own.at[g], v_own.at[g], 1, g, 2, own_send.at[1, g])

    def relay(index, g):
        source, slot, shift, _ = relays[index]
        return kv_copies(
            k_buf.at[source, g], v_buf.at[source, g], slot, g, shift, relay_send.at[index, g]
        )

    for g in range(groups):
        lanes = slice(g * TILE, (g + 1) * TILE)
        kcols = slice(width + g * TILE, width + (g + 1) * TILE)
        vcols = slice(2 * width + g * TILE, 2 * width + (g + 1) * TILE)
        k_own[g] = f32dot(h_s[...], w2_ref[:, kcols]).astype(jnp.bfloat16)
        v_own[g] = f32dot(h_s[...], w2_ref[:, vcols]).T.astype(jnp.bfloat16)

        @pl.when(to_chip)
        def _():
            for copy in own_chip(g):
                copy.start()

        @pl.when(to_next)
        def _():
            for copy in own_next(g):
                copy.start()

    for g in range(groups):
        lanes = slice(g * TILE, (g + 1) * TILE)
        qt_ref[lanes, :] = f32dot(h_s[...], w2_ref[:, lanes]).T.astype(jnp.bfloat16)

        @pl.when(helped)
        def _():
            query_back(g).start()

    tall = lax.broadcasted_iota(jnp.int32, (LANES, 1), 0) < LANES // 2
    scale = SCALE2 * 64 ** (-0.5)
    halves = rows // TILE
    per_group = TILE // LANES

    def attend(k_ref, v_ref, g, first, bias):
        def body(i, carry):
            p = i // halves
            hq = lax.rem(i, halves)
            lanes = tile_at(hq, TILE)
            query = qt_ref[tile_at(p + g * per_group, LANES), lanes]
            keys = k_ref[:, tile_at(p, LANES)]
            for half in range(2):
                keep = tall if half == 0 else jnp.logical_not(tall)
                mine = jnp.where(keep, query.astype(jnp.float32), 0.0).astype(jnp.bfloat16)
                s = f32dot(keys, mine) * scale
                if first:
                    seen = lax.broadcasted_iota(jnp.int32, s.shape, 0) <= (
                        lax.broadcasted_iota(jnp.int32, s.shape, 1) + hq * TILE
                    )
                    s = jnp.where(seen, s, -jnp.inf)
                top = jnp.max(s, axis=0, keepdims=True)
                h = 2 * (p + g * per_group) + half
                vrow = pl.ds(pl.multiple_of((2 * p + half) * 64, 64), 64)
                arow = pl.ds(pl.multiple_of(h * 64, 64), 64)
                if first:
                    m_new = top
                    ref_top = top
                else:
                    m_old = m_s[h, :, lanes]
                    m_new = jnp.maximum(m_old, top + bias)
                    ref_top = m_new - bias
                    alpha = jnp.exp2(m_old - m_new)
                w = jnp.exp2(s - ref_top)
                total = jnp.sum(w, axis=0, keepdims=True)
                part = f32dot(v_ref[vrow, :], w.astype(jnp.bfloat16))
                if first:
                    l_s[h, :, lanes] = total
                    acc_s[arow, lanes] = part
                else:
                    l_s[h, :, lanes] = l_s[h, :, lanes] * alpha + total
                    acc_s[arow, lanes] = acc_s[arow, lanes] * alpha + part
                m_s[h, :, lanes] = m_new
            return carry

        lax.fori_loop(0, per_group * halves, body, 0)

    def attend_far(k_ref, v_ref, g):
        def body(i, carry):
            p = i // halves
            lanes = tile_at(lax.rem(i, halves), TILE)
            query = q_far[tile_at(p + g * per_group, LANES), lanes]
            keys = k_ref[:, tile_at(p, LANES)]
            for half in range(2):
                keep = tall if half == 0 else jnp.logical_not(tall)
                mine = jnp.where(keep, query.astype(jnp.float32), 0.0).astype(jnp.bfloat16)
                s = f32dot(keys, mine) * scale
                top = jnp.max(s, axis=0, keepdims=True)
                w = jnp.exp2(s - top)
                total = jnp.sum(w, axis=0, keepdims=True)
                h = 2 * p + half
                vrow = pl.ds(pl.multiple_of(h * 64, 64), 64)
                part = f32dot(v_ref[vrow, :], w.astype(jnp.bfloat16))
                o_send[g, vrow, lanes] = (part * (1.0 / total)).astype(jnp.bfloat16)
                st_send[g, h, :, lanes] = top
                st_send[g, h + 2 * per_group, :, lanes] = total
            return carry

        lax.fori_loop(0, per_group * halves, body, 0)

    def merge(g, bias):
        for j in range(2 * per_group):
            h = 2 * per_group * g + j
            arow = slice(h * 64, (h + 1) * 64)
            m_old = m_s[h]
            m_far = st_recv[g, j] + bias
            m_new = jnp.maximum(m_old, m_far)
            alpha = jnp.exp2(m_old - m_new)
            beta = st_recv[g, j + 2 * per_group] * jnp.exp2(m_far - m_new)
            l_s[h] = l_s[h] * alpha + beta
            far = o_recv[g, j * 64 : (j + 1) * 64, :].astype(jnp.float32)
            acc_s[arow, :] = acc_s[arow, :] * alpha + far * beta

    def listing(slot):
        back = me - slot - 1
        listed = ids_ref[0, 0] == back
        for j in range(1, ids_ref.shape[1]):
            listed = jnp.logical_or(listed, ids_ref[0, j] == back)
        return jnp.where(listed, jnp.float32(0.0), jnp.float32(-jnp.inf))

    for g in range(groups):
        attend(k_own.at[g], v_own.at[g], g, True, None)

    order = [(slot, g) for g in range(groups) for slot in range(2)]
    order += [(2, g) for g in range(groups)]
    for slot, g in order:
        here = me >= slot + 1
        if slot == 2:
            here = jnp.logical_and(here, jnp.logical_not(even))

            @pl.when(helped)
            def _():
                for copy in partial_on(g):
                    copy.wait_recv()
                merge(g, listing(2))

        @pl.when(here)
        def _():
            for copy in kv_copies(k_own.at[g], v_own.at[g], slot, g, 0, own_send.at[0, g]):
                copy.wait_recv()
            for index in range(len(relays)):
                if relays[index][0] == slot:
                    @pl.when(relays[index][3])
                    def _():
                        for copy in relay(index, g):
                            copy.start()
            if slot == 0:
                @pl.when(helps)
                def _():
                    query_back(g).wait_recv()
                    attend_far(k_buf.at[0, g], v_buf.at[0, g], g)
                    for copy in partial_on(g):
                        copy.start()
            bias = listing(slot)
            attend(k_buf.at[slot, g], v_buf.at[slot, g], g, False, bias)

    for p in range(pairs):
        prow = slice(p * LANES, (p + 1) * LANES)
        inv = jnp.where(tall, 1.0 / l_s[2 * p], 1.0 / l_s[2 * p + 1])
        y_s[:, prow] = (acc_s[prow, :] * inv).T.astype(jnp.bfloat16)

    def last_tile(j, carry):
        cols = tile_at(j, TILE)
        branch = f32dot(y_s[...], wp_ref[:, cols])
        out_ref[:, cols] = (hid_ref[:, cols].astype(jnp.float32) + branch).astype(jnp.bfloat16)
        return carry

    loads[5].wait()
    lax.fori_loop(0, hid_ref.shape[1] // TILE, last_tile, 0)

    def drain(copies):
        for copy in copies:
            copy.wait_send()

    for r, dist in enumerate(dists):
        @pl.when(me + dist < n)
        def _():
            copy_of(r, dist).wait_send()

    for g in range(groups):
        @pl.when(to_next)
        def _():
            drain(own_next(g))

        @pl.when(to_chip)
        def _():
            drain(own_chip(g))

        @pl.when(helped)
        def _():
            query_back(g).wait_send()

        @pl.when(helps)
        def _():
            drain(partial_on(g))

        for index in range(len(relays)):
            @pl.when(relays[index][3])
            def _():
                drain(relay(index, g))


def local(
    frames, norm_gain1, w_qkv1, log_decay, head_gain, w_out1, norm_gain2, w_qkv2, window_ids, w_out2
):
    n = lax.axis_size("tm")
    rows, model = frames.shape
    width = w_out1.shape[0]
    heads = log_decay.shape[0]
    rounds = max(2, (n - 1).bit_length())
    groups = width // TILE
    vmem = pl.BlockSpec(memory_space=pltpu.VMEM)
    hbm = pl.BlockSpec(memory_space=pltpu.HBM)
    smem = pl.BlockSpec(memory_space=pltpu.SMEM)
    bf, f32 = jnp.bfloat16, jnp.float32
    return pl.pallas_call(
        functools.partial(both_layers, n),
        out_shape=jax.ShapeDtypeStruct((rows, model), bf),
        in_specs=[hbm, vmem, hbm, vmem, vmem, hbm, vmem, hbm, smem, hbm],
        out_specs=vmem,
        scratch_shapes=[
            pltpu.VMEM((rows, model), bf),
            pltpu.VMEM((model, 3 * width), bf),
            pltpu.VMEM((width, model), bf),
            pltpu.VMEM((model, 3 * width), bf),
            pltpu.VMEM((width, model), bf),
            pltpu.VMEM((rows, model), bf),
            pltpu.VMEM((width, rows), bf),
            pltpu.VMEM((groups, rows, TILE), bf),
            pltpu.VMEM((groups, TILE, rows), bf),
            pltpu.VMEM((3, groups, rows, TILE), bf),
            pltpu.VMEM((3, groups, TILE, rows), bf),
            pltpu.VMEM((heads, 1, rows), f32),
            pltpu.VMEM((heads, 1, rows), f32),
            pltpu.VMEM((width, rows), f32),
            pltpu.SemaphoreType.DMA((6,)),
            pltpu.SemaphoreType.DMA((2, groups, 2)),
            pltpu.SemaphoreType.DMA((2, groups, 2)),
            pltpu.SemaphoreType.DMA((3, groups, 2)),
            pltpu.VMEM((width, rows), bf),
            pltpu.VMEM((groups, TILE, rows), bf),
            pltpu.VMEM((groups, TILE, rows), bf),
            pltpu.VMEM((groups, heads, 1, rows), f32),
            pltpu.VMEM((groups, heads, 1, rows), f32),
            pltpu.SemaphoreType.DMA((groups, 3)),
            pltpu.SemaphoreType.DMA((groups, 3)),
            pltpu.VMEM((rows, model), bf),
            pltpu.VMEM((rows, 3 * width), bf),
            pltpu.VMEM((rows, width), bf),
            pltpu.VMEM((heads, rows), f32),
            pltpu.VMEM((rows, heads), f32),
            pltpu.VMEM((rows, width), f32),
            pltpu.VMEM((64, width), f32),
            pltpu.VMEM((1, width), f32),
            pltpu.VMEM((64, width), f32),
            pltpu.VMEM((1, width), f32),
            pltpu.VMEM((rounds, 80, width), bf),
            pltpu.VMEM((rounds, 80, width), bf),
            pltpu.SemaphoreType.DMA((rounds,)),
            pltpu.SemaphoreType.DMA((rounds,)),
        ],
        compiler_params=pltpu.CompilerParams(
            collective_id=0, has_side_effects=True, vmem_limit_bytes=60 * 2**20
        ),
    )(
        frames, norm_gain1.reshape(1, model), w_qkv1, log_decay, head_gain.reshape(1, width),
        w_out1, norm_gain2.reshape(1, model), w_qkv2, window_ids, w_out2,
    )


def solution(mesh):
    placed = (
        P(("dp", "tm"), None),
        P(),
        P(),
        P(None, ("dp", "tm")),
        P(),
        P(),
        P(),
        P(),
        P(("dp", "tm"), None),
        P(),
    )
    return jax.shard_map(
        local, mesh=mesh, in_specs=placed, out_specs=P(("dp", "tm"), None), check_vma=False
    )
```

```python
import functools

import jax
import jax.numpy as jnp
from jax import lax
from jax.experimental import pallas as pl
from jax.experimental.pallas import tpu as pltpu
from jax.sharding import PartitionSpec as P

MESH = pl.DeviceIdType.MESH
TILE = 256
LANES = 128
SCALE2 = 1.4426950408889634


def f32dot(a, b, dims=(((1,), (0,)), ((), ()))):
    return lax.dot_general(a, b, dims, preferred_element_type=jnp.float32)


def tile_at(index, size):
    return pl.ds(pl.multiple_of(index * size, size), size)


def norm_rows(src_ref, gain_ref, dst_ref):
    step = 128

    def body(i, carry):
        rows = tile_at(i, step)
        wide = src_ref[rows, :].astype(jnp.float32)
        scale = lax.rsqrt(jnp.mean(wide * wide, axis=-1, keepdims=True) + 1e-05)
        dst_ref[rows, :] = (wide * scale * gain_ref[...]).astype(jnp.bfloat16)
        return carry

    lax.fori_loop(0, src_ref.shape[0] // step, body, 0)


def both_layers(
    n,
    x_hbm, g1_ref, w1_hbm, ld_ref, hg_ref, wo_hbm, g2_ref, w2_hbm, ids_ref,
    hid_ref, attn_ref,
    x_ref, w1_ref, wo_ref, w2_ref, qt_ref, k_own, v_own, k_buf, v_buf,
    m_s, l_s, acc_s, load_sem, own_send, relay_send, kv_recv,
    q_far, o_send, o_recv, st_send, st_recv, far_send, far_recv,
    h_s, qkv_s, y_s, run_s, runt_s, lin_s, x_s, ax_s, e_s, a_s, send_b, recv_b, send_sem, recv_sem,
):
    me = lax.axis_index("tm")
    rows = x_ref.shape[0]
    width = wo_ref.shape[0]
    heads = ld_ref.shape[0]
    pairs = width // LANES
    rounds = max(2, (n - 1).bit_length())
    dists = [1 << r for r in range(rounds)]

    barrier = pltpu.get_barrier_semaphore()
    for dist in dists:
        @pl.when(me + dist < n)
        def _():
            pl.semaphore_signal(barrier, inc=1, device_id={"tm": me + dist}, device_id_type=MESH)

        @pl.when(me >= dist)
        def _():
            pl.semaphore_signal(barrier, inc=1, device_id={"tm": me - dist}, device_id_type=MESH)

    loads = [
        pltpu.make_async_copy(src, dst, load_sem.at[i])
        for i, (src, dst) in enumerate(
            [
                (x_hbm, x_ref),
                (w1_hbm.at[:, width:], w1_ref.at[:, width:]),
                (w1_hbm.at[:, :width], w1_ref.at[:, :width]),
                (wo_hbm, wo_ref),
                (w2_hbm, w2_ref),
            ]
        )
    ]
    for load in loads:
        load.start()
    loads[0].wait()
    norm_rows(x_ref, g1_ref, h_s)
    loads[1].wait()

    def project(j, carry):
        cols = tile_at(j, TILE)
        qkv_s[:, cols] = f32dot(h_s[...], w1_ref[:, cols]).astype(jnp.bfloat16)
        return carry

    lax.fori_loop(width // TILE, 3 * width // TILE, project, 0)

    upper = (
        lax.broadcasted_iota(jnp.int32, (rows, rows), 0)
        <= lax.broadcasted_iota(jnp.int32, (rows, rows), 1)
    ).astype(jnp.float32)
    run = lax.dot_general(
        ld_ref[...], upper, (((1,), (0,)), ((), ())),
        precision=lax.Precision.HIGHEST, preferred_element_type=jnp.float32,
    )
    run_s[...] = run
    runt_s[...] = run.T
    last = run[:, rows - 1 : rows]
    headsel = lax.broadcasted_iota(jnp.int32, (heads, width), 1) // (
        width // heads
    ) == lax.broadcasted_iota(jnp.int32, (heads, width), 0)
    a_row = jnp.sum(jnp.where(headsel, jnp.exp(last), 0.0), axis=0, keepdims=True)
    a_s[...] = a_row
    low = lax.broadcasted_iota(jnp.int32, (1, LANES), 1) < LANES // 2
    left_t = jnp.exp(last - run).T

    for p in range(pairs):
        cols = slice(p * LANES, (p + 1) * LANES)
        kcols = slice(width + p * LANES, width + (p + 1) * LANES)
        vcols = slice(2 * width + p * LANES, 2 * width + (p + 1) * LANES)
        decay = jnp.where(low, left_t[:, 2 * p : 2 * p + 1], left_t[:, 2 * p + 1 : 2 * p + 2])
        keyed = (qkv_s[:, kcols].astype(jnp.float32) * decay).T.astype(jnp.bfloat16)
        full = f32dot(keyed, qkv_s[:, vcols])
        e_s[:, cols] = jnp.where(low, full[: LANES // 2], full[LANES // 2 :])
    x_s[...] = jnp.zeros_like(x_s)
    ax_s[...] = jnp.ones_like(ax_s)

    def send(r, dist):
        w = e_s[...] + a_s[...] * x_s[...]
        aw = a_s[...] * ax_s[...]
        hi = aw.astype(jnp.bfloat16).astype(jnp.float32)
        lo = aw - hi
        row = lax.broadcasted_iota(jnp.int32, (16, width), 0)
        tail = jnp.where(row == 0, hi, jnp.where(row == 1, lo, 0.0))
        send_b[r, 0:64, :] = w.astype(jnp.bfloat16)
        send_b[r, 64:80, :] = tail.astype(jnp.bfloat16)

        @pl.when(me + dist < n)
        def _():
            copy_of(r, dist).start()

    def copy_of(r, dist):
        return pltpu.make_async_remote_copy(
            src_ref=send_b.at[r], dst_ref=recv_b.at[r],
            send_sem=send_sem.at[r], recv_sem=recv_sem.at[r],
            device_id={"tm": me + dist}, device_id_type=MESH,
        )

    def receive(r, dist):
        @pl.when(me >= dist)
        def _():
            copy_of(r, dist).wait_recv()
            got = recv_b[r].astype(jnp.float32)
            x_s[...] = x_s[...] + ax_s[...] * got[0:64]
            ax_s[...] = ax_s[...] * (got[64:65] + got[65:66])

    peers = [me + dist < n for dist in dists] + [me >= dist for dist in dists]
    pl.semaphore_wait(barrier, sum(peer.astype(jnp.int32) for peer in peers))

    def work_query():
        loads[2].wait()
        lax.fori_loop(0, width // TILE, project, 0)

    def work_pair(p):
        cols = slice(p * LANES, (p + 1) * LANES)
        kcols = slice(width + p * LANES, width + (p + 1) * LANES)
        vcols = slice(2 * width + p * LANES, 2 * width + (p + 1) * LANES)
        for first in range(0, rows, TILE):
            upto = first + TILE
            parts = []
            query = qkv_s[first:upto, cols]
            keys = qkv_s[0:upto, kcols]
            vals = qkv_s[0:upto, vcols]
            causal = lax.broadcasted_iota(jnp.int32, (TILE, upto), 0) + first >= (
                lax.broadcasted_iota(jnp.int32, (TILE, upto), 1)
            )
            for half in range(2):
                h = 2 * p + half
                keep = low if half == 0 else jnp.logical_not(low)
                mine = jnp.where(keep, query.astype(jnp.float32), 0.0).astype(jnp.bfloat16)
                scores = f32dot(mine, keys, (((1,), (1,)), ((), ())))
                diff = runt_s[first:upto, h : h + 1] - run_s[h : h + 1, 0:upto]
                weight = jnp.where(causal, jnp.exp(jnp.minimum(diff, 0.0)), 0.0)
                parts.append(f32dot((scores * weight).astype(jnp.bfloat16), vals))
            lin_s[first:upto, cols] = jnp.where(low, parts[0], parts[1])

    work = [work_query] + [functools.partial(work_pair, p) for p in range(pairs)]
    send(0, dists[0])
    for r, dist in enumerate(dists):
        take = 1 if r < rounds - 1 else len(work)
        if r == 1:
            take = 2
        for item in work[:take]:
            item()
        work = work[take:]
        receive(r, dist)
        if r + 1 < rounds:
            send(r + 1, dists[r + 1])
    for item in work:
        item()

    for p in range(pairs):
        cols = slice(p * LANES, (p + 1) * LANES)
        packed = x_s[:, cols]
        state = jnp.concatenate(
            [jnp.where(low, packed, 0.0), jnp.where(low, 0.0, packed)], axis=0
        ).astype(jnp.bfloat16)
        grow = jnp.exp(
            jnp.where(low, runt_s[:, 2 * p : 2 * p + 1], runt_s[:, 2 * p + 1 : 2 * p + 2])
        )
        scaled = (qkv_s[:, cols].astype(jnp.float32) * grow).astype(jnp.bfloat16)
        lin = lin_s[:, cols] + f32dot(scaled, state)
        square = lin * lin
        s0 = jnp.sum(jnp.where(low, square, 0.0), axis=-1, keepdims=True)
        s1 = jnp.sum(jnp.where(low, 0.0, square), axis=-1, keepdims=True)
        mean = jnp.where(low, s0, s1) * (1.0 / 64)
        y_s[:, cols] = (lin * lax.rsqrt(mean + 1e-06) * hg_ref[:, cols]).astype(jnp.bfloat16)

    def out_tile(j, carry):
        cols = tile_at(j, TILE)
        branch = f32dot(y_s[...], wo_ref[:, cols])
        hid_ref[:, cols] = (x_ref[:, cols].astype(jnp.float32) + branch).astype(jnp.bfloat16)
        return carry

    loads[3].wait()
    lax.fori_loop(0, x_ref.shape[1] // TILE, out_tile, 0)
    loads[4].wait()
    norm_rows(hid_ref, g2_ref, h_s)

    groups = width // TILE
    even = lax.rem(me, 2) == 0
    to_next = me + 1 < n
    to_chip = jnp.logical_and(even, me + 2 < n)
    relays = [
        (0, 1, 1, jnp.logical_and(even, jnp.logical_and(me >= 1, to_next))),
        (1, 2, 1, jnp.logical_and(even, jnp.logical_and(me >= 2, to_next))),
    ]
    helps = jnp.logical_and(to_chip, me >= 1)
    helped = jnp.logical_and(even, me >= 3)

    def query_back(g):
        return pltpu.make_async_remote_copy(
            src_ref=qt_ref.at[tile_at(g, TILE)], dst_ref=q_far.at[tile_at(g, TILE)],
            send_sem=far_send.at[g, 0], recv_sem=far_recv.at[g, 0],
            device_id={"tm": me - 2}, device_id_type=MESH,
        )

    def partial_on(g):
        return [
            pltpu.make_async_remote_copy(
                src_ref=src.at[g], dst_ref=dst.at[g],
                send_sem=far_send.at[g, i], recv_sem=far_recv.at[g, i],
                device_id={"tm": me + 2}, device_id_type=MESH,
            )
            for i, (src, dst) in [(1, (o_send, o_recv)), (2, (st_send, st_recv))]
        ]

    def kv_copies(keys, vals, slot, g, shift, sems):
        return [
            pltpu.make_async_remote_copy(
                src_ref=src, dst_ref=dst.at[slot, g], send_sem=sems.at[i],
                recv_sem=kv_recv.at[slot, g, i],
                device_id={"tm": me + shift}, device_id_type=MESH,
            )
            for i, (src, dst) in enumerate([(keys, k_buf), (vals, v_buf)])
        ]

    def own_next(g):
        return kv_copies(k_own.at[g], v_own.at[g], 0, g, 1, own_send.at[0, g])

    def own_chip(g):
        return kv_copies(k_own.at[g], v_own.at[g], 1, g, 2, own_send.at[1, g])

    def relay(index, g):
        source, slot, shift, _ = relays[index]
        return kv_copies(
            k_buf.at[source, g], v_buf.at[source, g], slot, g, shift, relay_send.at[index, g]
        )

    for g in range(groups):
        lanes = slice(g * TILE, (g + 1) * TILE)
        kcols = slice(width + g * TILE, width + (g + 1) * TILE)
        vcols = slice(2 * width + g * TILE, 2 * width + (g + 1) * TILE)
        k_own[g] = f32dot(h_s[...], w2_ref[:, kcols]).astype(jnp.bfloat16)
        v_own[g] = f32dot(h_s[...], w2_ref[:, vcols]).T.astype(jnp.bfloat16)

        @pl.when(to_chip)
        def _():
            for copy in own_chip(g):
                copy.start()

        @pl.when(to_next)
        def _():
            for copy in own_next(g):
                copy.start()

    for g in range(groups):
        lanes = slice(g * TILE, (g + 1) * TILE)
        block = f32dot(h_s[...], w2_ref[:, lanes]) * (SCALE2 * 64 ** (-0.5))
        qt_ref[lanes, :] = block.T.astype(jnp.bfloat16)

        @pl.when(helped)
        def _():
            query_back(g).start()

    tall = lax.broadcasted_iota(jnp.int32, (LANES, 1), 0) < LANES // 2
    halves = rows // TILE
    per_group = TILE // LANES

    def attend(k_ref, v_ref, g, first, bias):
        def body(i, carry):
            p = i // halves
            hq = lax.rem(i, halves)
            lanes = tile_at(hq, TILE)
            query = qt_ref[tile_at(p + g * per_group, LANES), lanes]
            keys = k_ref[:, tile_at(p, LANES)]
            for half in range(2):
                keep = tall if half == 0 else jnp.logical_not(tall)
                mine = jnp.where(keep, query.astype(jnp.float32), 0.0).astype(jnp.bfloat16)
                s = f32dot(keys, mine)
                if first:
                    seen = lax.broadcasted_iota(jnp.int32, s.shape, 0) <= (
                        lax.broadcasted_iota(jnp.int32, s.shape, 1) + hq * TILE
                    )
                    s = jnp.where(seen, s, -jnp.inf)
                top = jnp.max(s, axis=0, keepdims=True)
                h = 2 * (p + g * per_group) + half
                vrow = pl.ds(pl.multiple_of((2 * p + half) * 64, 64), 64)
                arow = pl.ds(pl.multiple_of(h * 64, 64), 64)
                if first:
                    m_new = top
                    ref_top = top
                else:
                    m_old = m_s[h, :, lanes]
                    m_new = jnp.maximum(m_old, top + bias)
                    ref_top = m_new - bias
                    alpha = jnp.exp2(m_old - m_new)
                w = jnp.exp2(s - ref_top)
                total = jnp.sum(w, axis=0, keepdims=True)
                part = f32dot(v_ref[vrow, :], w.astype(jnp.bfloat16))
                if first:
                    l_s[h, :, lanes] = total
                    acc_s[arow, lanes] = part
                else:
                    l_s[h, :, lanes] = l_s[h, :, lanes] * alpha + total
                    acc_s[arow, lanes] = acc_s[arow, lanes] * alpha + part
                m_s[h, :, lanes] = m_new
            return carry

        lax.fori_loop(0, per_group * halves, body, 0)

    def attend_far(k_ref, v_ref, g):
        def body(i, carry):
            p = i // halves
            lanes = tile_at(lax.rem(i, halves), TILE)
            query = q_far[tile_at(p + g * per_group, LANES), lanes]
            keys = k_ref[:, tile_at(p, LANES)]
            for half in range(2):
                keep = tall if half == 0 else jnp.logical_not(tall)
                mine = jnp.where(keep, query.astype(jnp.float32), 0.0).astype(jnp.bfloat16)
                s = f32dot(keys, mine)
                top = jnp.max(s, axis=0, keepdims=True)
                w = jnp.exp2(s - top)
                total = jnp.sum(w, axis=0, keepdims=True)
                h = 2 * p + half
                vrow = pl.ds(pl.multiple_of(h * 64, 64), 64)
                part = f32dot(v_ref[vrow, :], w.astype(jnp.bfloat16))
                o_send[g, vrow, lanes] = (part * (1.0 / total)).astype(jnp.bfloat16)
                st_send[g, h, :, lanes] = top
                st_send[g, h + 2 * per_group, :, lanes] = total
            return carry

        lax.fori_loop(0, per_group * halves, body, 0)

    def merge(g, bias):
        for j in range(2 * per_group):
            h = 2 * per_group * g + j
            arow = slice(h * 64, (h + 1) * 64)
            m_old = m_s[h]
            m_far = st_recv[g, j] + bias
            m_new = jnp.maximum(m_old, m_far)
            alpha = jnp.exp2(m_old - m_new)
            beta = st_recv[g, j + 2 * per_group] * jnp.exp2(m_far - m_new)
            l_s[h] = l_s[h] * alpha + beta
            far = o_recv[g, j * 64 : (j + 1) * 64, :].astype(jnp.float32)
            acc_s[arow, :] = acc_s[arow, :] * alpha + far * beta

    def listing(slot):
        back = me - slot - 1
        listed = ids_ref[0, 0] == back
        for j in range(1, ids_ref.shape[1]):
            listed = jnp.logical_or(listed, ids_ref[0, j] == back)
        return jnp.where(listed, jnp.float32(0.0), jnp.float32(-jnp.inf))

    for g in range(groups):
        attend(k_own.at[g], v_own.at[g], g, True, None)

    def arrive(slot, g):
        for copy in kv_copies(k_own.at[g], v_own.at[g], slot, g, 0, own_send.at[0, g]):
            copy.wait_recv()
        for index in range(len(relays)):
            if relays[index][0] == slot:
                @pl.when(relays[index][3])
                def _():
                    for copy in relay(index, g):
                        copy.start()

    def attend_slot(slot, g):
        attend(k_buf.at[slot, g], v_buf.at[slot, g], g, False, listing(slot))

    for g in range(groups):
        @pl.when(me >= 1)
        def _():
            arrive(0, g)

            @pl.when(helps)
            def _():
                query_back(g).wait_recv()
                attend_far(k_buf.at[0, g], v_buf.at[0, g], g)
                for copy in partial_on(g):
                    copy.start()

        @pl.when(me >= 2)
        def _():
            arrive(1, g)

        for slot in range(2):
            @pl.when(me >= slot + 1)
            def _():
                attend_slot(slot, g)

    for g in range(groups):
        @pl.when(helped)
        def _():
            for copy in partial_on(g):
                copy.wait_recv()
            merge(g, listing(2))

        @pl.when(jnp.logical_and(me >= 3, jnp.logical_not(even)))
        def _():
            arrive(2, g)
            attend_slot(2, g)

    for p in range(pairs):
        prow = slice(p * LANES, (p + 1) * LANES)
        inv = jnp.where(tall, 1.0 / l_s[2 * p], 1.0 / l_s[2 * p + 1])
        attn_ref[:, prow] = (acc_s[prow, :] * inv).T.astype(jnp.bfloat16)

    def drain(copies):
        for copy in copies:
            copy.wait_send()

    for r, dist in enumerate(dists):
        @pl.when(me + dist < n)
        def _():
            copy_of(r, dist).wait_send()

    for g in range(groups):
        @pl.when(to_next)
        def _():
            drain(own_next(g))

        @pl.when(to_chip)
        def _():
            drain(own_chip(g))

        @pl.when(helped)
        def _():
            query_back(g).wait_send()

        @pl.when(helps)
        def _():
            drain(partial_on(g))

        for index in range(len(relays)):
            @pl.when(relays[index][3])
            def _():
                drain(relay(index, g))


def local(
    frames, norm_gain1, w_qkv1, log_decay, head_gain, w_out1, norm_gain2, w_qkv2, window_ids, w_out2
):
    n = lax.axis_size("tm")
    rows, model = frames.shape
    width = w_out1.shape[0]
    heads = log_decay.shape[0]
    rounds = max(2, (n - 1).bit_length())
    groups = width // TILE
    vmem = pl.BlockSpec(memory_space=pltpu.VMEM)
    hbm = pl.BlockSpec(memory_space=pltpu.HBM)
    smem = pl.BlockSpec(memory_space=pltpu.SMEM)
    bf, f32 = jnp.bfloat16, jnp.float32
    hidden1, attn = pl.pallas_call(
        functools.partial(both_layers, n),
        out_shape=(
            jax.ShapeDtypeStruct((rows, model), bf),
            jax.ShapeDtypeStruct((rows, width), bf),
        ),
        in_specs=[hbm, vmem, hbm, vmem, vmem, hbm, vmem, hbm, smem],
        out_specs=(vmem, vmem),
        scratch_shapes=[
            pltpu.VMEM((rows, model), bf),
            pltpu.VMEM((model, 3 * width), bf),
            pltpu.VMEM((width, model), bf),
            pltpu.VMEM((model, 3 * width), bf),
            pltpu.VMEM((width, rows), bf),
            pltpu.VMEM((groups, rows, TILE), bf),
            pltpu.VMEM((groups, TILE, rows), bf),
            pltpu.VMEM((3, groups, rows, TILE), bf),
            pltpu.VMEM((3, groups, TILE, rows), bf),
            pltpu.VMEM((heads, 1, rows), f32),
            pltpu.VMEM((heads, 1, rows), f32),
            pltpu.VMEM((width, rows), f32),
            pltpu.SemaphoreType.DMA((5,)),
            pltpu.SemaphoreType.DMA((2, groups, 2)),
            pltpu.SemaphoreType.DMA((2, groups, 2)),
            pltpu.SemaphoreType.DMA((3, groups, 2)),
            pltpu.VMEM((width, rows), bf),
            pltpu.VMEM((groups, TILE, rows), bf),
            pltpu.VMEM((groups, TILE, rows), bf),
            pltpu.VMEM((groups, heads, 1, rows), f32),
            pltpu.VMEM((groups, heads, 1, rows), f32),
            pltpu.SemaphoreType.DMA((groups, 3)),
            pltpu.SemaphoreType.DMA((groups, 3)),
            pltpu.VMEM((rows, model), bf),
            pltpu.VMEM((rows, 3 * width), bf),
            pltpu.VMEM((rows, width), bf),
            pltpu.VMEM((heads, rows), f32),
            pltpu.VMEM((rows, heads), f32),
            pltpu.VMEM((rows, width), f32),
            pltpu.VMEM((64, width), f32),
            pltpu.VMEM((1, width), f32),
            pltpu.VMEM((64, width), f32),
            pltpu.VMEM((1, width), f32),
            pltpu.VMEM((rounds, 80, width), bf),
            pltpu.VMEM((rounds, 80, width), bf),
            pltpu.SemaphoreType.DMA((rounds,)),
            pltpu.SemaphoreType.DMA((rounds,)),
        ],
        compiler_params=pltpu.CompilerParams(
            collective_id=0, has_side_effects=True, vmem_limit_bytes=60 * 2**20
        ),
    )(
        frames, norm_gain1.reshape(1, model), w_qkv1, log_decay, head_gain.reshape(1, width),
        w_out1, norm_gain2.reshape(1, model), w_qkv2, window_ids,
    )
    branch = jnp.dot(attn, w_out2, preferred_element_type=jnp.float32)
    return (hidden1.astype(jnp.float32) + branch).astype(jnp.bfloat16)


def solution(mesh):
    placed = (
        P(("dp", "tm"), None),
        P(),
        P(),
        P(None, ("dp", "tm")),
        P(),
        P(),
        P(),
        P(),
        P(("dp", "tm"), None),
        P(),
    )
    return jax.shard_map(
        local, mesh=mesh, in_specs=placed, out_specs=P(("dp", "tm"), None), check_vma=False
    )
```

```python
import functools

import jax
import jax.numpy as jnp
from jax import lax
from jax.experimental import pallas as pl
from jax.experimental.pallas import tpu as pltpu
from jax.sharding import PartitionSpec as P

MESH = pl.DeviceIdType.MESH
TILE = 256
LANES = 128
SCALE2 = 1.4426950408889634


def f32dot(a, b, dims=(((1,), (0,)), ((), ()))):
    return lax.dot_general(a, b, dims, preferred_element_type=jnp.float32)


def tile_at(index, size):
    return pl.ds(pl.multiple_of(index * size, size), size)


def norm_rows(src_ref, gain_ref, dst_ref):
    step = 128

    def body(i, carry):
        rows = tile_at(i, step)
        wide = src_ref[rows, :].astype(jnp.float32)
        scale = lax.rsqrt(jnp.mean(wide * wide, axis=-1, keepdims=True) + 1e-05)
        dst_ref[rows, :] = (wide * scale * gain_ref[...]).astype(jnp.bfloat16)
        return carry

    lax.fori_loop(0, src_ref.shape[0] // step, body, 0)


def both_layers(
    n,
    x_hbm, g1_ref, w1_hbm, ld_ref, hg_ref, wo_hbm, g2_ref, w2_hbm, ids_ref, wp_hbm,
    out_ref,
    x_ref, w1_ref, wo_ref, w2_ref, wp_ref, hid_ref, qt_ref, k_own, v_own, k_buf, v_buf,
    m_s, l_s, acc_s, load_sem, own_send, relay_send, kv_recv,
    q_far, o_send, o_recv, st_send, st_recv, far_send, far_recv,
    h_s, qkv_s, y_s, run_s, runt_s, lin_s, x_s, ax_s, e_s, a_s, send_b, recv_b, send_sem, recv_sem,
):
    me = lax.axis_index("tm")
    rows = x_ref.shape[0]
    width = wo_ref.shape[0]
    heads = ld_ref.shape[0]
    pairs = width // LANES
    rounds = max(2, (n - 1).bit_length())
    dists = [1 << r for r in range(rounds)]

    barrier = pltpu.get_barrier_semaphore()
    for dist in dists:
        @pl.when(me + dist < n)
        def _():
            pl.semaphore_signal(barrier, inc=1, device_id={"tm": me + dist}, device_id_type=MESH)

        @pl.when(me >= dist)
        def _():
            pl.semaphore_signal(barrier, inc=1, device_id={"tm": me - dist}, device_id_type=MESH)

    loads = [
        pltpu.make_async_copy(src, dst, load_sem.at[i])
        for i, (src, dst) in enumerate(
            [
                (x_hbm, x_ref),
                (w1_hbm.at[:, width:], w1_ref.at[:, width:]),
                (w1_hbm.at[:, :width], w1_ref.at[:, :width]),
                (wo_hbm, wo_ref),
                (w2_hbm, w2_ref),
                (wp_hbm, wp_ref),
            ]
        )
    ]
    for load in loads:
        load.start()
    loads[0].wait()
    norm_rows(x_ref, g1_ref, h_s)
    loads[1].wait()

    def project(j, carry):
        cols = tile_at(j, TILE)
        qkv_s[:, cols] = f32dot(h_s[...], w1_ref[:, cols]).astype(jnp.bfloat16)
        return carry

    lax.fori_loop(width // TILE, 3 * width // TILE, project, 0)

    upper = (
        lax.broadcasted_iota(jnp.int32, (rows, rows), 0)
        <= lax.broadcasted_iota(jnp.int32, (rows, rows), 1)
    ).astype(jnp.float32)
    run = lax.dot_general(
        ld_ref[...], upper, (((1,), (0,)), ((), ())),
        precision=lax.Precision.HIGHEST, preferred_element_type=jnp.float32,
    )
    run_s[...] = run
    runt_s[...] = run.T
    last = run[:, rows - 1 : rows]
    headsel = lax.broadcasted_iota(jnp.int32, (heads, width), 1) // (
        width // heads
    ) == lax.broadcasted_iota(jnp.int32, (heads, width), 0)
    a_row = jnp.sum(jnp.where(headsel, jnp.exp(last), 0.0), axis=0, keepdims=True)
    a_s[...] = a_row
    low = lax.broadcasted_iota(jnp.int32, (1, LANES), 1) < LANES // 2
    left_t = jnp.exp(last - run).T

    for p in range(pairs):
        cols = slice(p * LANES, (p + 1) * LANES)
        kcols = slice(width + p * LANES, width + (p + 1) * LANES)
        vcols = slice(2 * width + p * LANES, 2 * width + (p + 1) * LANES)
        decay = jnp.where(low, left_t[:, 2 * p : 2 * p + 1], left_t[:, 2 * p + 1 : 2 * p + 2])
        keyed = (qkv_s[:, kcols].astype(jnp.float32) * decay).T.astype(jnp.bfloat16)
        full = f32dot(keyed, qkv_s[:, vcols])
        e_s[:, cols] = jnp.where(low, full[: LANES // 2], full[LANES // 2 :])
    x_s[...] = jnp.zeros_like(x_s)
    ax_s[...] = jnp.ones_like(ax_s)

    def send(r, dist):
        w = e_s[...] + a_s[...] * x_s[...]
        aw = a_s[...] * ax_s[...]
        hi = aw.astype(jnp.bfloat16).astype(jnp.float32)
        lo = aw - hi
        row = lax.broadcasted_iota(jnp.int32, (16, width), 0)
        tail = jnp.where(row == 0, hi, jnp.where(row == 1, lo, 0.0))
        send_b[r, 0:64, :] = w.astype(jnp.bfloat16)
        send_b[r, 64:80, :] = tail.astype(jnp.bfloat16)

        @pl.when(me + dist < n)
        def _():
            copy_of(r, dist).start()

    def copy_of(r, dist):
        return pltpu.make_async_remote_copy(
            src_ref=send_b.at[r], dst_ref=recv_b.at[r],
            send_sem=send_sem.at[r], recv_sem=recv_sem.at[r],
            device_id={"tm": me + dist}, device_id_type=MESH,
        )

    def receive(r, dist):
        @pl.when(me >= dist)
        def _():
            copy_of(r, dist).wait_recv()
            got = recv_b[r].astype(jnp.float32)
            x_s[...] = x_s[...] + ax_s[...] * got[0:64]
            ax_s[...] = ax_s[...] * (got[64:65] + got[65:66])

    peers = [me + dist < n for dist in dists] + [me >= dist for dist in dists]
    pl.semaphore_wait(barrier, sum(peer.astype(jnp.int32) for peer in peers))

    def work_query():
        loads[2].wait()
        lax.fori_loop(0, width // TILE, project, 0)

    def work_pair(p):
        cols = slice(p * LANES, (p + 1) * LANES)
        kcols = slice(width + p * LANES, width + (p + 1) * LANES)
        vcols = slice(2 * width + p * LANES, 2 * width + (p + 1) * LANES)
        for first in range(0, rows, TILE):
            upto = first + TILE
            parts = []
            query = qkv_s[first:upto, cols]
            keys = qkv_s[0:upto, kcols]
            vals = qkv_s[0:upto, vcols]
            causal = lax.broadcasted_iota(jnp.int32, (TILE, upto), 0) + first >= (
                lax.broadcasted_iota(jnp.int32, (TILE, upto), 1)
            )
            for half in range(2):
                h = 2 * p + half
                keep = low if half == 0 else jnp.logical_not(low)
                mine = jnp.where(keep, query.astype(jnp.float32), 0.0).astype(jnp.bfloat16)
                scores = f32dot(mine, keys, (((1,), (1,)), ((), ())))
                diff = runt_s[first:upto, h : h + 1] - run_s[h : h + 1, 0:upto]
                weight = jnp.where(causal, jnp.exp(jnp.minimum(diff, 0.0)), 0.0)
                parts.append(f32dot((scores * weight).astype(jnp.bfloat16), vals))
            lin_s[first:upto, cols] = jnp.where(low, parts[0], parts[1])

    work = [work_query] + [functools.partial(work_pair, p) for p in range(pairs)]
    send(0, dists[0])
    for r, dist in enumerate(dists):
        take = 1 if r < rounds - 1 else len(work)
        if r == 1:
            take = 2
        for item in work[:take]:
            item()
        work = work[take:]
        receive(r, dist)
        if r + 1 < rounds:
            send(r + 1, dists[r + 1])
    for item in work:
        item()

    for p in range(pairs):
        cols = slice(p * LANES, (p + 1) * LANES)
        packed = x_s[:, cols]
        state = jnp.concatenate(
            [jnp.where(low, packed, 0.0), jnp.where(low, 0.0, packed)], axis=0
        ).astype(jnp.bfloat16)
        grow = jnp.exp(
            jnp.where(low, runt_s[:, 2 * p : 2 * p + 1], runt_s[:, 2 * p + 1 : 2 * p + 2])
        )
        scaled = (qkv_s[:, cols].astype(jnp.float32) * grow).astype(jnp.bfloat16)
        lin = lin_s[:, cols] + f32dot(scaled, state)
        square = lin * lin
        s0 = jnp.sum(jnp.where(low, square, 0.0), axis=-1, keepdims=True)
        s1 = jnp.sum(jnp.where(low, 0.0, square), axis=-1, keepdims=True)
        mean = jnp.where(low, s0, s1) * (1.0 / 64)
        y_s[:, cols] = (lin * lax.rsqrt(mean + 1e-06) * hg_ref[:, cols]).astype(jnp.bfloat16)

    def out_tile(j, carry):
        cols = tile_at(j, TILE)
        branch = f32dot(y_s[...], wo_ref[:, cols])
        hid_ref[:, cols] = (x_ref[:, cols].astype(jnp.float32) + branch).astype(jnp.bfloat16)
        return carry

    loads[3].wait()
    lax.fori_loop(0, x_ref.shape[1] // TILE, out_tile, 0)
    loads[4].wait()
    norm_rows(hid_ref, g2_ref, h_s)

    groups = width // TILE
    even = lax.rem(me, 2) == 0
    to_next = me + 1 < n
    to_chip = jnp.logical_and(even, me + 2 < n)
    relays = [
        (0, 1, 1, jnp.logical_and(even, jnp.logical_and(me >= 1, to_next))),
        (1, 2, 1, jnp.logical_and(even, jnp.logical_and(me >= 2, to_next))),
    ]
    helps = jnp.logical_and(to_chip, me >= 1)
    helped = jnp.logical_and(even, me >= 3)

    def query_back(g):
        return pltpu.make_async_remote_copy(
            src_ref=qt_ref.at[tile_at(g, TILE)], dst_ref=q_far.at[tile_at(g, TILE)],
            send_sem=far_send.at[g, 0], recv_sem=far_recv.at[g, 0],
            device_id={"tm": me - 2}, device_id_type=MESH,
        )

    def partial_on(g):
        return [
            pltpu.make_async_remote_copy(
                src_ref=src.at[g], dst_ref=dst.at[g],
                send_sem=far_send.at[g, i], recv_sem=far_recv.at[g, i],
                device_id={"tm": me + 2}, device_id_type=MESH,
            )
            for i, (src, dst) in [(1, (o_send, o_recv)), (2, (st_send, st_recv))]
        ]

    def kv_copies(keys, vals, slot, g, shift, sems):
        return [
            pltpu.make_async_remote_copy(
                src_ref=src, dst_ref=dst.at[slot, g], send_sem=sems.at[i],
                recv_sem=kv_recv.at[slot, g, i],
                device_id={"tm": me + shift}, device_id_type=MESH,
            )
            for i, (src, dst) in enumerate([(keys, k_buf), (vals, v_buf)])
        ]

    def own_next(g):
        return kv_copies(k_own.at[g], v_own.at[g], 0, g, 1, own_send.at[0, g])

    def own_chip(g):
        return kv_copies(k_own.at[g], v_own.at[g], 1, g, 2, own_send.at[1, g])

    def relay(index, g):
        source, slot, shift, _ = relays[index]
        return kv_copies(
            k_buf.at[source, g], v_buf.at[source, g], slot, g, shift, relay_send.at[index, g]
        )

    for g in range(groups):
        lanes = slice(g * TILE, (g + 1) * TILE)
        kcols = slice(width + g * TILE, width + (g + 1) * TILE)
        vcols = slice(2 * width + g * TILE, 2 * width + (g + 1) * TILE)
        k_own[g] = f32dot(h_s[...], w2_ref[:, kcols]).astype(jnp.bfloat16)
        v_own[g] = f32dot(h_s[...], w2_ref[:, vcols]).T.astype(jnp.bfloat16)

        @pl.when(to_chip)
        def _():
            for copy in own_chip(g):
                copy.start()

        @pl.when(to_next)
        def _():
            for copy in own_next(g):
                copy.start()

    for g in range(groups):
        lanes = slice(g * TILE, (g + 1) * TILE)
        block = f32dot(h_s[...], w2_ref[:, lanes]) * (SCALE2 * 64 ** (-0.5))
        qt_ref[lanes, :] = block.T.astype(jnp.bfloat16)

        @pl.when(helped)
        def _():
            query_back(g).start()

    tall = lax.broadcasted_iota(jnp.int32, (LANES, 1), 0) < LANES // 2
    halves = rows // TILE
    per_group = TILE // LANES

    def attend(k_ref, v_ref, g, first, bias):
        def body(i, carry):
            p = i // halves
            hq = lax.rem(i, halves)
            lanes = tile_at(hq, TILE)
            query = qt_ref[tile_at(p + g * per_group, LANES), lanes]
            keys = k_ref[:, tile_at(p, LANES)]
            for half in range(2):
                keep = tall if half == 0 else jnp.logical_not(tall)
                mine = jnp.where(keep, query.astype(jnp.float32), 0.0).astype(jnp.bfloat16)
                s = f32dot(keys, mine)
                if first:
                    seen = lax.broadcasted_iota(jnp.int32, s.shape, 0) <= (
                        lax.broadcasted_iota(jnp.int32, s.shape, 1) + hq * TILE
                    )
                    s = jnp.where(seen, s, -jnp.inf)
                top = jnp.max(s, axis=0, keepdims=True)
                h = 2 * (p + g * per_group) + half
                vrow = pl.ds(pl.multiple_of((2 * p + half) * 64, 64), 64)
                arow = pl.ds(pl.multiple_of(h * 64, 64), 64)
                if first:
                    m_new = top
                    ref_top = top
                else:
                    m_old = m_s[h, :, lanes]
                    m_new = jnp.maximum(m_old, top + bias)
                    ref_top = m_new - bias
                    alpha = jnp.exp2(m_old - m_new)
                w = jnp.exp2(s - ref_top)
                total = jnp.sum(w, axis=0, keepdims=True)
                part = f32dot(v_ref[vrow, :], w.astype(jnp.bfloat16))
                if first:
                    l_s[h, :, lanes] = total
                    acc_s[arow, lanes] = part
                else:
                    l_s[h, :, lanes] = l_s[h, :, lanes] * alpha + total
                    acc_s[arow, lanes] = acc_s[arow, lanes] * alpha + part
                m_s[h, :, lanes] = m_new
            return carry

        lax.fori_loop(0, per_group * halves, body, 0)

    def attend_far(k_ref, v_ref, g):
        def body(i, carry):
            p = i // halves
            lanes = tile_at(lax.rem(i, halves), TILE)
            query = q_far[tile_at(p + g * per_group, LANES), lanes]
            keys = k_ref[:, tile_at(p, LANES)]
            for half in range(2):
                keep = tall if half == 0 else jnp.logical_not(tall)
                mine = jnp.where(keep, query.astype(jnp.float32), 0.0).astype(jnp.bfloat16)
                s = f32dot(keys, mine)
                top = jnp.max(s, axis=0, keepdims=True)
                w = jnp.exp2(s - top)
                total = jnp.sum(w, axis=0, keepdims=True)
                h = 2 * p + half
                vrow = pl.ds(pl.multiple_of(h * 64, 64), 64)
                part = f32dot(v_ref[vrow, :], w.astype(jnp.bfloat16))
                o_send[g, vrow, lanes] = (part * (1.0 / total)).astype(jnp.bfloat16)
                st_send[g, h, :, lanes] = top
                st_send[g, h + 2 * per_group, :, lanes] = total
            return carry

        lax.fori_loop(0, per_group * halves, body, 0)

    def merge(g, bias):
        for j in range(2 * per_group):
            h = 2 * per_group * g + j
            arow = slice(h * 64, (h + 1) * 64)
            m_old = m_s[h]
            m_far = st_recv[g, j] + bias
            m_new = jnp.maximum(m_old, m_far)
            alpha = jnp.exp2(m_old - m_new)
            beta = st_recv[g, j + 2 * per_group] * jnp.exp2(m_far - m_new)
            l_s[h] = l_s[h] * alpha + beta
            far = o_recv[g, j * 64 : (j + 1) * 64, :].astype(jnp.float32)
            acc_s[arow, :] = acc_s[arow, :] * alpha + far * beta

    def listing(slot):
        back = me - slot - 1
        listed = ids_ref[0, 0] == back
        for j in range(1, ids_ref.shape[1]):
            listed = jnp.logical_or(listed, ids_ref[0, j] == back)
        return jnp.where(listed, jnp.float32(0.0), jnp.float32(-jnp.inf))

    for g in range(groups):
        attend(k_own.at[g], v_own.at[g], g, True, None)

    odd = jnp.logical_not(even)

    def arrive(slot, g):
        for copy in kv_copies(k_own.at[g], v_own.at[g], slot, g, 0, own_send.at[0, g]):
            copy.wait_recv()
        for index in range(len(relays)):
            if relays[index][0] == slot:
                @pl.when(relays[index][3])
                def _():
                    for copy in relay(index, g):
                        copy.start()

    def attend_slot(slot, g):
        attend(k_buf.at[slot, g], v_buf.at[slot, g], g, False, listing(slot))

    @pl.when(odd)
    def _():
        for g in range(groups):
            arrive(0, g)
            attend_slot(0, g)
        for g in range(groups):
            for slot in (1, 2):
                @pl.when(me >= slot + 1)
                def _():
                    arrive(slot, g)
                    attend_slot(slot, g)

    @pl.when(jnp.logical_and(even, me >= 2))
    def _():
        for g in range(groups):
            arrive(0, g)
            arrive(1, g)

            @pl.when(helps)
            def _():
                query_back(g).wait_recv()
                attend_far(k_buf.at[0, g], v_buf.at[0, g], g)
                for copy in partial_on(g):
                    copy.start()

            attend_slot(0, g)
            attend_slot(1, g)

    for g in range(groups):
        @pl.when(helped)
        def _():
            for copy in partial_on(g):
                copy.wait_recv()
            merge(g, listing(2))

    for p in range(pairs):
        prow = slice(p * LANES, (p + 1) * LANES)
        inv = jnp.where(tall, 1.0 / l_s[2 * p], 1.0 / l_s[2 * p + 1])
        y_s[:, prow] = (acc_s[prow, :] * inv).T.astype(jnp.bfloat16)

    def last_tile(j, carry):
        cols = tile_at(j, TILE)
        branch = f32dot(y_s[...], wp_ref[:, cols])
        out_ref[:, cols] = (hid_ref[:, cols].astype(jnp.float32) + branch).astype(jnp.bfloat16)
        return carry

    loads[5].wait()
    lax.fori_loop(0, hid_ref.shape[1] // TILE, last_tile, 0)

    def drain(copies):
        for copy in copies:
            copy.wait_send()

    for r, dist in enumerate(dists):
        @pl.when(me + dist < n)
        def _():
            copy_of(r, dist).wait_send()

    for g in range(groups):
        @pl.when(to_next)
        def _():
            drain(own_next(g))

        @pl.when(to_chip)
        def _():
            drain(own_chip(g))

        @pl.when(helped)
        def _():
            query_back(g).wait_send()

        @pl.when(helps)
        def _():
            drain(partial_on(g))

        for index in range(len(relays)):
            @pl.when(relays[index][3])
            def _():
                drain(relay(index, g))


def local(
    frames, norm_gain1, w_qkv1, log_decay, head_gain, w_out1, norm_gain2, w_qkv2, window_ids, w_out2
):
    n = lax.axis_size("tm")
    rows, model = frames.shape
    width = w_out1.shape[0]
    heads = log_decay.shape[0]
    rounds = max(2, (n - 1).bit_length())
    groups = width // TILE
    vmem = pl.BlockSpec(memory_space=pltpu.VMEM)
    hbm = pl.BlockSpec(memory_space=pltpu.HBM)
    smem = pl.BlockSpec(memory_space=pltpu.SMEM)
    bf, f32 = jnp.bfloat16, jnp.float32
    return pl.pallas_call(
        functools.partial(both_layers, n),
        out_shape=jax.ShapeDtypeStruct((rows, model), bf),
        in_specs=[hbm, vmem, hbm, vmem, vmem, hbm, vmem, hbm, smem, hbm],
        out_specs=vmem,
        scratch_shapes=[
            pltpu.VMEM((rows, model), bf),
            pltpu.VMEM((model, 3 * width), bf),
            pltpu.VMEM((width, model), bf),
            pltpu.VMEM((model, 3 * width), bf),
            pltpu.VMEM((width, model), bf),
            pltpu.VMEM((rows, model), bf),
            pltpu.VMEM((width, rows), bf),
            pltpu.VMEM((groups, rows, TILE), bf),
            pltpu.VMEM((groups, TILE, rows), bf),
            pltpu.VMEM((3, groups, rows, TILE), bf),
            pltpu.VMEM((3, groups, TILE, rows), bf),
            pltpu.VMEM((heads, 1, rows), f32),
            pltpu.VMEM((heads, 1, rows), f32),
            pltpu.VMEM((width, rows), f32),
            pltpu.SemaphoreType.DMA((6,)),
            pltpu.SemaphoreType.DMA((2, groups, 2)),
            pltpu.SemaphoreType.DMA((2, groups, 2)),
            pltpu.SemaphoreType.DMA((3, groups, 2)),
            pltpu.VMEM((width, rows), bf),
            pltpu.VMEM((groups, TILE, rows), bf),
            pltpu.VMEM((groups, TILE, rows), bf),
            pltpu.VMEM((groups, heads, 1, rows), f32),
            pltpu.VMEM((groups, heads, 1, rows), f32),
            pltpu.SemaphoreType.DMA((groups, 3)),
            pltpu.SemaphoreType.DMA((groups, 3)),
            pltpu.VMEM((rows, model), bf),
            pltpu.VMEM((rows, 3 * width), bf),
            pltpu.VMEM((rows, width), bf),
            pltpu.VMEM((heads, rows), f32),
            pltpu.VMEM((rows, heads), f32),
            pltpu.VMEM((rows, width), f32),
            pltpu.VMEM((64, width), f32),
            pltpu.VMEM((1, width), f32),
            pltpu.VMEM((64, width), f32),
            pltpu.VMEM((1, width), f32),
            pltpu.VMEM((rounds, 80, width), bf),
            pltpu.VMEM((rounds, 80, width), bf),
            pltpu.SemaphoreType.DMA((rounds,)),
            pltpu.SemaphoreType.DMA((rounds,)),
        ],
        compiler_params=pltpu.CompilerParams(
            collective_id=0, has_side_effects=True, vmem_limit_bytes=60 * 2**20
        ),
    )(
        frames, norm_gain1.reshape(1, model), w_qkv1, log_decay, head_gain.reshape(1, width),
        w_out1, norm_gain2.reshape(1, model), w_qkv2, window_ids, w_out2,
    )


def solution(mesh):
    placed = (
        P(("dp", "tm"), None),
        P(),
        P(),
        P(None, ("dp", "tm")),
        P(),
        P(),
        P(),
        P(),
        P(("dp", "tm"), None),
        P(),
    )
    return jax.shard_map(
        local, mesh=mesh, in_specs=placed, out_specs=P(("dp", "tm"), None), check_vma=False
    )
```

```python
import functools

import jax
import jax.numpy as jnp
from jax import lax
from jax.experimental import pallas as pl
from jax.experimental.pallas import tpu as pltpu
from jax.sharding import PartitionSpec as P

MESH = pl.DeviceIdType.MESH
TILE = 256
LANES = 128
SCALE2 = 1.4426950408889634


def f32dot(a, b, dims=(((1,), (0,)), ((), ()))):
    return lax.dot_general(a, b, dims, preferred_element_type=jnp.float32)


def tile_at(index, size):
    return pl.ds(pl.multiple_of(index * size, size), size)


def norm_rows(src_ref, gain_ref, dst_ref):
    step = 128

    def body(i, carry):
        rows = tile_at(i, step)
        wide = src_ref[rows, :].astype(jnp.float32)
        scale = lax.rsqrt(jnp.mean(wide * wide, axis=-1, keepdims=True) + 1e-05)
        dst_ref[rows, :] = (wide * scale * gain_ref[...]).astype(jnp.bfloat16)
        return carry

    lax.fori_loop(0, src_ref.shape[0] // step, body, 0)


def both_layers(
    n,
    x_hbm, g1_ref, w1_hbm, ld_ref, hg_ref, wo_hbm, g2_ref, w2_hbm, ids_ref, wp_hbm,
    out_ref,
    x_ref, w1_ref, wo_ref, w2_ref, wp_ref, hid_ref, qt_ref, k_own, v_own, k_buf, v_buf,
    m_s, l_s, acc_s, load_sem, own_send, relay_send, kv_recv,
    q_far, o_send, o_recv, st_send, st_recv, far_send, far_recv,
    h_s, qkv_s, y_s, run_s, runt_s, lin_s, x_s, ax_s, e_s, a_s, send_b, recv_b, send_sem, recv_sem,
):
    me = lax.axis_index("tm")
    rows = x_ref.shape[0]
    width = wo_ref.shape[0]
    heads = ld_ref.shape[0]
    pairs = width // LANES
    rounds = max(2, (n - 1).bit_length())
    dists = [1 << r for r in range(rounds)]

    barrier = pltpu.get_barrier_semaphore()
    for dist in dists:
        @pl.when(me + dist < n)
        def _():
            pl.semaphore_signal(barrier, inc=1, device_id={"tm": me + dist}, device_id_type=MESH)

        @pl.when(me >= dist)
        def _():
            pl.semaphore_signal(barrier, inc=1, device_id={"tm": me - dist}, device_id_type=MESH)

    loads = [
        pltpu.make_async_copy(src, dst, load_sem.at[i])
        for i, (src, dst) in enumerate(
            [
                (x_hbm, x_ref),
                (w1_hbm.at[:, width:], w1_ref.at[:, width:]),
                (w1_hbm.at[:, :width], w1_ref.at[:, :width]),
                (wo_hbm, wo_ref),
                (w2_hbm, w2_ref),
                (wp_hbm, wp_ref),
            ]
        )
    ]
    for load in loads:
        load.start()
    loads[0].wait()
    norm_rows(x_ref, g1_ref, h_s)
    loads[1].wait()

    def project(j, carry):
        cols = tile_at(j, TILE)
        qkv_s[:, cols] = f32dot(h_s[...], w1_ref[:, cols]).astype(jnp.bfloat16)
        return carry

    lax.fori_loop(width // TILE, 3 * width // TILE, project, 0)

    upper = (
        lax.broadcasted_iota(jnp.int32, (rows, rows), 0)
        <= lax.broadcasted_iota(jnp.int32, (rows, rows), 1)
    ).astype(jnp.float32)
    run = lax.dot_general(
        ld_ref[...], upper, (((1,), (0,)), ((), ())),
        precision=lax.Precision.HIGHEST, preferred_element_type=jnp.float32,
    )
    run_s[...] = run
    runt_s[...] = run.T
    last = run[:, rows - 1 : rows]
    headsel = lax.broadcasted_iota(jnp.int32, (heads, width), 1) // (
        width // heads
    ) == lax.broadcasted_iota(jnp.int32, (heads, width), 0)
    a_row = jnp.sum(jnp.where(headsel, jnp.exp(last), 0.0), axis=0, keepdims=True)
    a_s[...] = a_row
    low = lax.broadcasted_iota(jnp.int32, (1, LANES), 1) < LANES // 2
    left_t = jnp.exp(last - run).T

    for p in range(pairs):
        cols = slice(p * LANES, (p + 1) * LANES)
        kcols = slice(width + p * LANES, width + (p + 1) * LANES)
        vcols = slice(2 * width + p * LANES, 2 * width + (p + 1) * LANES)
        decay = jnp.where(low, left_t[:, 2 * p : 2 * p + 1], left_t[:, 2 * p + 1 : 2 * p + 2])
        keyed = (qkv_s[:, kcols].astype(jnp.float32) * decay).T.astype(jnp.bfloat16)
        full = f32dot(keyed, qkv_s[:, vcols])
        e_s[:, cols] = jnp.where(low, full[: LANES // 2], full[LANES // 2 :])
    x_s[...] = jnp.zeros_like(x_s)
    ax_s[...] = jnp.ones_like(ax_s)

    def send(r, dist):
        w = e_s[...] + a_s[...] * x_s[...]
        aw = a_s[...] * ax_s[...]
        hi = aw.astype(jnp.bfloat16).astype(jnp.float32)
        lo = aw - hi
        row = lax.broadcasted_iota(jnp.int32, (16, width), 0)
        tail = jnp.where(row == 0, hi, jnp.where(row == 1, lo, 0.0))
        send_b[r, 0:64, :] = w.astype(jnp.bfloat16)
        send_b[r, 64:80, :] = tail.astype(jnp.bfloat16)

        @pl.when(me + dist < n)
        def _():
            copy_of(r, dist).start()

    def copy_of(r, dist):
        return pltpu.make_async_remote_copy(
            src_ref=send_b.at[r], dst_ref=recv_b.at[r],
            send_sem=send_sem.at[r], recv_sem=recv_sem.at[r],
            device_id={"tm": me + dist}, device_id_type=MESH,
        )

    def receive(r, dist):
        @pl.when(me >= dist)
        def _():
            copy_of(r, dist).wait_recv()
            got = recv_b[r].astype(jnp.float32)
            x_s[...] = x_s[...] + ax_s[...] * got[0:64]
            ax_s[...] = ax_s[...] * (got[64:65] + got[65:66])

    peers = [me + dist < n for dist in dists] + [me >= dist for dist in dists]
    pl.semaphore_wait(barrier, sum(peer.astype(jnp.int32) for peer in peers))

    def work_query():
        loads[2].wait()
        lax.fori_loop(0, width // TILE, project, 0)

    def work_pair(p):
        cols = slice(p * LANES, (p + 1) * LANES)
        kcols = slice(width + p * LANES, width + (p + 1) * LANES)
        vcols = slice(2 * width + p * LANES, 2 * width + (p + 1) * LANES)
        for first in range(0, rows, TILE):
            upto = first + TILE
            parts = []
            query = qkv_s[first:upto, cols]
            keys = qkv_s[0:upto, kcols]
            vals = qkv_s[0:upto, vcols]
            causal = lax.broadcasted_iota(jnp.int32, (TILE, upto), 0) + first >= (
                lax.broadcasted_iota(jnp.int32, (TILE, upto), 1)
            )
            for half in range(2):
                h = 2 * p + half
                keep = low if half == 0 else jnp.logical_not(low)
                mine = jnp.where(keep, query.astype(jnp.float32), 0.0).astype(jnp.bfloat16)
                scores = f32dot(mine, keys, (((1,), (1,)), ((), ())))
                diff = runt_s[first:upto, h : h + 1] - run_s[h : h + 1, 0:upto]
                weight = jnp.where(causal, jnp.exp(jnp.minimum(diff, 0.0)), 0.0)
                parts.append(f32dot((scores * weight).astype(jnp.bfloat16), vals))
            lin_s[first:upto, cols] = jnp.where(low, parts[0], parts[1])

    work = [work_query] + [functools.partial(work_pair, p) for p in range(pairs)]
    send(0, dists[0])
    for r, dist in enumerate(dists):
        take = 1 if r < rounds - 1 else len(work)
        if r == 1:
            take = 2
        for item in work[:take]:
            item()
        work = work[take:]
        receive(r, dist)
        if r + 1 < rounds:
            send(r + 1, dists[r + 1])
    for item in work:
        item()

    for p in range(pairs):
        cols = slice(p * LANES, (p + 1) * LANES)
        packed = x_s[:, cols]
        state = jnp.concatenate(
            [jnp.where(low, packed, 0.0), jnp.where(low, 0.0, packed)], axis=0
        ).astype(jnp.bfloat16)
        grow = jnp.exp(
            jnp.where(low, runt_s[:, 2 * p : 2 * p + 1], runt_s[:, 2 * p + 1 : 2 * p + 2])
        )
        scaled = (qkv_s[:, cols].astype(jnp.float32) * grow).astype(jnp.bfloat16)
        lin = lin_s[:, cols] + f32dot(scaled, state)
        square = lin * lin
        s0 = jnp.sum(jnp.where(low, square, 0.0), axis=-1, keepdims=True)
        s1 = jnp.sum(jnp.where(low, 0.0, square), axis=-1, keepdims=True)
        mean = jnp.where(low, s0, s1) * (1.0 / 64)
        y_s[:, cols] = (lin * lax.rsqrt(mean + 1e-06) * hg_ref[:, cols]).astype(jnp.bfloat16)

    def out_tile(j, carry):
        cols = tile_at(j, TILE)
        branch = f32dot(y_s[...], wo_ref[:, cols])
        hid_ref[:, cols] = (x_ref[:, cols].astype(jnp.float32) + branch).astype(jnp.bfloat16)
        return carry

    loads[3].wait()
    lax.fori_loop(0, x_ref.shape[1] // TILE, out_tile, 0)
    loads[4].wait()
    norm_rows(hid_ref, g2_ref, h_s)

    groups = width // TILE
    even = lax.rem(me, 2) == 0
    to_next = me + 1 < n
    to_chip = jnp.logical_and(even, me + 2 < n)
    relays = [
        (0, 1, 1, jnp.logical_and(even, jnp.logical_and(me >= 1, to_next))),
        (1, 2, 1, jnp.logical_and(even, jnp.logical_and(me >= 2, to_next))),
    ]
    helps = jnp.logical_and(to_chip, me >= 1)
    helped = jnp.logical_and(even, me >= 3)

    def query_back(g):
        return pltpu.make_async_remote_copy(
            src_ref=qt_ref.at[tile_at(g, TILE)], dst_ref=q_far.at[tile_at(g, TILE)],
            send_sem=far_send.at[g, 0], recv_sem=far_recv.at[g, 0],
            device_id={"tm": me - 2}, device_id_type=MESH,
        )

    def partial_on(g):
        return [
            pltpu.make_async_remote_copy(
                src_ref=src.at[g], dst_ref=dst.at[g],
                send_sem=far_send.at[g, i], recv_sem=far_recv.at[g, i],
                device_id={"tm": me + 2}, device_id_type=MESH,
            )
            for i, (src, dst) in [(1, (o_send, o_recv)), (2, (st_send, st_recv))]
        ]

    def kv_copies(keys, vals, slot, g, shift, sems):
        return [
            pltpu.make_async_remote_copy(
                src_ref=src, dst_ref=dst.at[slot, g], send_sem=sems.at[i],
                recv_sem=kv_recv.at[slot, g, i],
                device_id={"tm": me + shift}, device_id_type=MESH,
            )
            for i, (src, dst) in enumerate([(keys, k_buf), (vals, v_buf)])
        ]

    def own_next(g):
        return kv_copies(k_own.at[g], v_own.at[g], 0, g, 1, own_send.at[0, g])

    def own_chip(g):
        return kv_copies(k_own.at[g], v_own.at[g], 1, g, 2, own_send.at[1, g])

    def relay(index, g):
        source, slot, shift, _ = relays[index]
        return kv_copies(
            k_buf.at[source, g], v_buf.at[source, g], slot, g, shift, relay_send.at[index, g]
        )

    for g in range(groups):
        lanes = slice(g * TILE, (g + 1) * TILE)
        kcols = slice(width + g * TILE, width + (g + 1) * TILE)
        vcols = slice(2 * width + g * TILE, 2 * width + (g + 1) * TILE)
        k_own[g] = f32dot(h_s[...], w2_ref[:, kcols]).astype(jnp.bfloat16)
        v_own[g] = f32dot(h_s[...], w2_ref[:, vcols]).T.astype(jnp.bfloat16)

        @pl.when(to_chip)
        def _():
            for copy in own_chip(g):
                copy.start()

        @pl.when(to_next)
        def _():
            for copy in own_next(g):
                copy.start()

    for g in range(groups):
        lanes = slice(g * TILE, (g + 1) * TILE)
        block = f32dot(h_s[...], w2_ref[:, lanes]) * (SCALE2 * 64 ** (-0.5))
        qt_ref[lanes, :] = block.T.astype(jnp.bfloat16)

        @pl.when(helped)
        def _():
            query_back(g).start()

    tall = lax.broadcasted_iota(jnp.int32, (LANES, 1), 0) < LANES // 2
    halves = rows // TILE
    per_group = TILE // LANES

    def attend(k_ref, v_ref, g, first, bias):
        def body(i, carry):
            p = i // halves
            hq = lax.rem(i, halves)
            lanes = tile_at(hq, TILE)
            query = qt_ref[tile_at(p + g * per_group, LANES), lanes]
            keys = k_ref[:, tile_at(p, LANES)]
            for half in range(2):
                keep = tall if half == 0 else jnp.logical_not(tall)
                mine = jnp.where(keep, query.astype(jnp.float32), 0.0).astype(jnp.bfloat16)
                s = f32dot(keys, mine)
                if first:
                    seen = lax.broadcasted_iota(jnp.int32, s.shape, 0) <= (
                        lax.broadcasted_iota(jnp.int32, s.shape, 1) + hq * TILE
                    )
                    s = jnp.where(seen, s, -jnp.inf)
                top = jnp.max(s, axis=0, keepdims=True)
                h = 2 * (p + g * per_group) + half
                vrow = pl.ds(pl.multiple_of((2 * p + half) * 64, 64), 64)
                arow = pl.ds(pl.multiple_of(h * 64, 64), 64)
                if first:
                    m_new = top
                    ref_top = top
                else:
                    m_old = m_s[h, :, lanes]
                    m_new = jnp.maximum(m_old, top + bias)
                    ref_top = m_new - bias
                    alpha = jnp.exp2(m_old - m_new)
                w = jnp.exp2(s - ref_top)
                total = jnp.sum(w, axis=0, keepdims=True)
                part = f32dot(v_ref[vrow, :], w.astype(jnp.bfloat16))
                if first:
                    l_s[h, :, lanes] = total
                    acc_s[arow, lanes] = part
                else:
                    l_s[h, :, lanes] = l_s[h, :, lanes] * alpha + total
                    acc_s[arow, lanes] = acc_s[arow, lanes] * alpha + part
                m_s[h, :, lanes] = m_new
            return carry

        lax.fori_loop(0, per_group * halves, body, 0)

    def attend_far(k_ref, v_ref, g):
        def body(i, carry):
            p = i // halves
            lanes = tile_at(lax.rem(i, halves), TILE)
            query = q_far[tile_at(p + g * per_group, LANES), lanes]
            keys = k_ref[:, tile_at(p, LANES)]
            for half in range(2):
                keep = tall if half == 0 else jnp.logical_not(tall)
                mine = jnp.where(keep, query.astype(jnp.float32), 0.0).astype(jnp.bfloat16)
                s = f32dot(keys, mine)
                top = jnp.max(s, axis=0, keepdims=True)
                w = jnp.exp2(s - top)
                total = jnp.sum(w, axis=0, keepdims=True)
                h = 2 * p + half
                vrow = pl.ds(pl.multiple_of(h * 64, 64), 64)
                part = f32dot(v_ref[vrow, :], w.astype(jnp.bfloat16))
                o_send[g, vrow, lanes] = (part * (1.0 / total)).astype(jnp.bfloat16)
                st_send[g, h, :, lanes] = top
                st_send[g, h + 2 * per_group, :, lanes] = total
            return carry

        lax.fori_loop(0, per_group * halves, body, 0)

    def merge(g, bias):
        for j in range(2 * per_group):
            h = 2 * per_group * g + j
            arow = slice(h * 64, (h + 1) * 64)
            m_old = m_s[h]
            m_far = st_recv[g, j] + bias
            m_new = jnp.maximum(m_old, m_far)
            alpha = jnp.exp2(m_old - m_new)
            beta = st_recv[g, j + 2 * per_group] * jnp.exp2(m_far - m_new)
            l_s[h] = l_s[h] * alpha + beta
            far = o_recv[g, j * 64 : (j + 1) * 64, :].astype(jnp.float32)
            acc_s[arow, :] = acc_s[arow, :] * alpha + far * beta

    def listing(slot):
        back = me - slot - 1
        listed = ids_ref[0, 0] == back
        for j in range(1, ids_ref.shape[1]):
            listed = jnp.logical_or(listed, ids_ref[0, j] == back)
        return jnp.where(listed, jnp.float32(0.0), jnp.float32(-jnp.inf))

    for g in range(groups):
        attend(k_own.at[g], v_own.at[g], g, True, None)

    odd = jnp.logical_not(even)

    def arrive(slot, g):
        for copy in kv_copies(k_own.at[g], v_own.at[g], slot, g, 0, own_send.at[0, g]):
            copy.wait_recv()
        for index in range(len(relays)):
            if relays[index][0] == slot:
                @pl.when(relays[index][3])
                def _():
                    for copy in relay(index, g):
                        copy.start()

    def attend_slot(slot, g):
        attend(k_buf.at[slot, g], v_buf.at[slot, g], g, False, listing(slot))

    @pl.when(odd)
    def _():
        for g in range(groups):
            arrive(0, g)
            attend_slot(0, g)
        for g in range(groups):
            for slot in (1, 2):
                @pl.when(me >= slot + 1)
                def _():
                    arrive(slot, g)
                    attend_slot(slot, g)

    @pl.when(jnp.logical_and(even, me >= 2))
    def _():
        for g in range(groups):
            arrive(0, g)

            @pl.when(helps)
            def _():
                query_back(g).wait_recv()
                attend_far(k_buf.at[0, g], v_buf.at[0, g], g)
                for copy in partial_on(g):
                    copy.start()

            arrive(1, g)
            attend_slot(0, g)
            attend_slot(1, g)

    for g in range(groups):
        @pl.when(helped)
        def _():
            for copy in partial_on(g):
                copy.wait_recv()
            merge(g, listing(2))

    for p in range(pairs):
        prow = slice(p * LANES, (p + 1) * LANES)
        inv = jnp.where(tall, 1.0 / l_s[2 * p], 1.0 / l_s[2 * p + 1])
        y_s[:, prow] = (acc_s[prow, :] * inv).T.astype(jnp.bfloat16)

    def last_tile(j, carry):
        cols = tile_at(j, TILE)
        branch = f32dot(y_s[...], wp_ref[:, cols])
        out_ref[:, cols] = (hid_ref[:, cols].astype(jnp.float32) + branch).astype(jnp.bfloat16)
        return carry

    loads[5].wait()
    lax.fori_loop(0, hid_ref.shape[1] // TILE, last_tile, 0)

    def drain(copies):
        for copy in copies:
            copy.wait_send()

    for r, dist in enumerate(dists):
        @pl.when(me + dist < n)
        def _():
            copy_of(r, dist).wait_send()

    for g in range(groups):
        @pl.when(to_next)
        def _():
            drain(own_next(g))

        @pl.when(to_chip)
        def _():
            drain(own_chip(g))

        @pl.when(helped)
        def _():
            query_back(g).wait_send()

        @pl.when(helps)
        def _():
            drain(partial_on(g))

        for index in range(len(relays)):
            @pl.when(relays[index][3])
            def _():
                drain(relay(index, g))


def local(
    frames, norm_gain1, w_qkv1, log_decay, head_gain, w_out1, norm_gain2, w_qkv2, window_ids, w_out2
):
    n = lax.axis_size("tm")
    rows, model = frames.shape
    width = w_out1.shape[0]
    heads = log_decay.shape[0]
    rounds = max(2, (n - 1).bit_length())
    groups = width // TILE
    vmem = pl.BlockSpec(memory_space=pltpu.VMEM)
    hbm = pl.BlockSpec(memory_space=pltpu.HBM)
    smem = pl.BlockSpec(memory_space=pltpu.SMEM)
    bf, f32 = jnp.bfloat16, jnp.float32
    return pl.pallas_call(
        functools.partial(both_layers, n),
        out_shape=jax.ShapeDtypeStruct((rows, model), bf),
        in_specs=[hbm, vmem, hbm, vmem, vmem, hbm, vmem, hbm, smem, hbm],
        out_specs=vmem,
        scratch_shapes=[
            pltpu.VMEM((rows, model), bf),
            pltpu.VMEM((model, 3 * width), bf),
            pltpu.VMEM((width, model), bf),
            pltpu.VMEM((model, 3 * width), bf),
            pltpu.VMEM((width, model), bf),
            pltpu.VMEM((rows, model), bf),
            pltpu.VMEM((width, rows), bf),
            pltpu.VMEM((groups, rows, TILE), bf),
            pltpu.VMEM((groups, TILE, rows), bf),
            pltpu.VMEM((3, groups, rows, TILE), bf),
            pltpu.VMEM((3, groups, TILE, rows), bf),
            pltpu.VMEM((heads, 1, rows), f32),
            pltpu.VMEM((heads, 1, rows), f32),
            pltpu.VMEM((width, rows), f32),
            pltpu.SemaphoreType.DMA((6,)),
            pltpu.SemaphoreType.DMA((2, groups, 2)),
            pltpu.SemaphoreType.DMA((2, groups, 2)),
            pltpu.SemaphoreType.DMA((3, groups, 2)),
            pltpu.VMEM((width, rows), bf),
            pltpu.VMEM((groups, TILE, rows), bf),
            pltpu.VMEM((groups, TILE, rows), bf),
            pltpu.VMEM((groups, heads, 1, rows), f32),
            pltpu.VMEM((groups, heads, 1, rows), f32),
            pltpu.SemaphoreType.DMA((groups, 3)),
            pltpu.SemaphoreType.DMA((groups, 3)),
            pltpu.VMEM((rows, model), bf),
            pltpu.VMEM((rows, 3 * width), bf),
            pltpu.VMEM((rows, width), bf),
            pltpu.VMEM((heads, rows), f32),
            pltpu.VMEM((rows, heads), f32),
            pltpu.VMEM((rows, width), f32),
            pltpu.VMEM((64, width), f32),
            pltpu.VMEM((1, width), f32),
            pltpu.VMEM((64, width), f32),
            pltpu.VMEM((1, width), f32),
            pltpu.VMEM((rounds, 80, width), bf),
            pltpu.VMEM((rounds, 80, width), bf),
            pltpu.SemaphoreType.DMA((rounds,)),
            pltpu.SemaphoreType.DMA((rounds,)),
        ],
        compiler_params=pltpu.CompilerParams(
            collective_id=0, has_side_effects=True, vmem_limit_bytes=60 * 2**20
        ),
    )(
        frames, norm_gain1.reshape(1, model), w_qkv1, log_decay, head_gain.reshape(1, width),
        w_out1, norm_gain2.reshape(1, model), w_qkv2, window_ids, w_out2,
    )


def solution(mesh):
    placed = (
        P(("dp", "tm"), None),
        P(),
        P(),
        P(None, ("dp", "tm")),
        P(),
        P(),
        P(),
        P(),
        P(("dp", "tm"), None),
        P(),
    )
    return jax.shard_map(
        local, mesh=mesh, in_specs=placed, out_specs=P(("dp", "tm"), None), check_vma=False
    )
```
